32 devices in a mesh: group: 2 (over y), lon: 4 (over z), lat: 2 (over x), fld: 2 (over core).
Axes of the slice: x: 2, y: 2, z: 4, core: 2. Of those that a mesh axis runs over, the one named last changes fastest.
Arguments:
- background: float32 [8, 32, 8192], P('group', ('lat', 'fld'), 'lon'), parts along dimension 0, may hold values from -7.2 to 7.2
- decay_sq: float32 [4, 32, 8192], P(None, ('lat', 'fld'), 'lon'), may hold values from 0.02 to 0.5
- edge_weight: float32 [4, 32, 8192], P(None, ('lat', 'fld'), 'lon'), may hold values from 0.1 to 1
- coupling: float32 [4, 4], replicated, may hold values from -0.32 to 1.6, as said below
- obs_tiles: bfloat16 [256, 256, 256], P(('lon', 'lat', 'fld')), may hold values from -0.375 to 0.375
- obs_values: float32 [512, 256], P(('group', 'lon', 'lat', 'fld')), parts along dimension 0, may hold values from -15 to 15
- obs_weights: float32 [256, 256], P(('lon', 'lat', 'fld')), may hold values from 4 to 32
- obs_counts: int32 [256], P(('lon', 'lat', 'fld')), may hold values from 32 to 256, as said below
- swath_ids: int32 [256], P(('lon', 'lat', 'fld')), may hold values from 0 to 7
- swath_scale: float32 [8], replicated, may hold values from 0.5 to 2
- tile_owner: int32 [256], P(('lon', 'lat', 'fld')), may hold values from 0 to 3, as said below
- tile_slot: int32 [256], P(('lon', 'lat', 'fld')), may hold values from 0 to 255
Outputs:
- solution: float32 [8, 32, 8192], P('group', ('lat', 'fld'), 'lon'), parts along dimension 0
- residual: float32 [8, 32, 8192], P('group', ('lat', 'fld'), 'lon'), parts along dimension 0
The draws below stay inside these ranges and needn't reach their ends.
There are 2 independent parts, one for each index of `group`. The reference program is written for one: setup_inputs(seed, part) draws one part's arguments, and reference() takes and returns one part's arrays. A program takes and returns all parts, laid end to end along the dimension named above; an argument that names none is the same for every part. Nothing has to cross between parts.
Inputs may be any that keep to these rules, and one draw needn't show every extreme that they name: `obs_counts`: each device's 16 tiles include one with all 256 observations live. `tile_owner`: of one device's 16 tiles at most 4 read patches in any one longitude block, and in every block row some longitude block is read by exactly 4 tiles of each device of that block row. `coupling`: Symmetric, each diagonal entry above the sum of the magnitudes of its row's others.
All inputs are finite; a program needn't handle non-finite values.
Results may differ from the reference program's by a relative error of at most 0.0065.
Values may be sent and summed in bfloat16 or wider, within the bound.
A program may use at most 64 MiB of HBM per device.

```python
import math
import jax
import jax.numpy as jnp
from jax import lax

F = 4
DIRS = 4
PATCH = 256
OBS = 256
CAP = 4
SWATHS = 8
ITERS = 3
CLAT = 8
CLON = 2048
TILE_DEV = 16
LON_DEVS = 4
ROW_DEVS = 4
NLAT = 32
NLON = 8192
TILES = 256
NPATCH_DEV = 256


def draw_background(key, part):
    key_rows, key_values = jax.random.split(jax.random.fold_in(key, 5))
    lon_pos = jnp.arange(NLON).astype(jnp.float32)
    ramp = 1.0 + 2.0 * lon_pos / NLON
    row_scale = jnp.exp(jax.random.uniform(key_rows, (NLAT,), jnp.float32, 0.0, math.log(10.0)))
    values = jax.random.truncated_normal(key_values, -4.0, 4.0, (F, NLAT, NLON), jnp.float32)
    return 0.06 * row_scale[None, :, None] * values * ramp[None, None, :]


def draw_coupling(key, part):
    key_off, key_diagonal = jax.random.split(jax.random.fold_in(key, 7))
    drawn = jax.random.uniform(key_off, (F, F), jnp.float32, -0.32, 0.32)
    symmetric = 0.5 * (drawn + drawn.T)
    diagonal = jax.random.uniform(key_diagonal, (F,), jnp.float32, 1.0, 1.6)
    identity = jnp.eye(F, dtype=jnp.float32)
    return symmetric * (1.0 - identity) + identity * diagonal[None, :]


def draw_obs_counts(key, part):
    key_counts, key_full = jax.random.split(jax.random.fold_in(key, 11))
    counts = jax.random.randint(key_counts, (TILES,), OBS // 8, OBS + 1)
    blocks = TILES // TILE_DEV
    chosen = jax.random.randint(key_full, (blocks,), 0, TILE_DEV)
    within = jnp.arange(TILES) % TILE_DEV
    owner_block = jnp.arange(TILES) // TILE_DEV
    return jnp.where(within == chosen[owner_block], OBS, counts).astype(jnp.int32)


def draw_tile_owner(key, part):
    key_hot, key_pool, key_shuffle = jax.random.split(jax.random.fold_in(key, 23), 3)
    blocks = TILES // TILE_DEV
    hottest = jax.random.randint(key_hot, (ROW_DEVS,), 0, LON_DEVS)
    block_hot = hottest[jnp.arange(blocks) % ROW_DEVS]
    pool_size = (LON_DEVS - 1) * CAP
    pool_keys = jax.random.split(key_pool, blocks)
    picked = jax.vmap(lambda member_key: jax.random.permutation(member_key, pool_size))(pool_keys)[:, :TILE_DEV - CAP]
    others = (block_hot[:, None] + 1 + picked // CAP) % LON_DEVS
    assigned = jnp.concatenate([jnp.broadcast_to(block_hot[:, None], (blocks, CAP)), others], axis=1)
    shuffle_keys = jax.random.split(key_shuffle, blocks)
    shuffle = jax.vmap(lambda member_key: jax.random.permutation(member_key, TILE_DEV))(shuffle_keys)
    return jnp.take_along_axis(assigned, shuffle, axis=1).reshape(-1).astype(jnp.int32)


def with_ends(result, key, low, largest):
    spot = [jax.random.randint(jax.random.fold_in(key, axis), (), 0, length) for axis, length in enumerate(result.shape)]
    widest = result.shape.index(max(result.shape))
    beside = spot[:widest] + [(spot[widest] + 1) % result.shape[widest]] + spot[widest + 1:]
    return result.at[tuple(spot)].set(low).at[tuple(beside)].set(largest)


def steps_of(key, shape, cuts, low, top_value):
    level = 1.0
    for dim, blocks in cuts:
        steps = jax.random.uniform(jax.random.fold_in(jax.random.fold_in(key, 6), dim), (blocks,), jnp.float32, low / len(cuts), top_value / len(cuts))
        level = level * jnp.repeat(jnp.exp(steps), shape[dim] // blocks).reshape((-1,) + (1,) * (len(shape) - 1 - dim))
    return level


def bell_draw(own_key, dims, width, most, cuts=(), kind=jnp.bfloat16):
    result = width * jax.random.normal(own_key, dims, jnp.float32)
    if cuts:
        result = result * steps_of(own_key, dims, cuts, -0.22, 0.18)
    return jnp.clip(result, -most, most).astype(kind)


def setup_inputs(seed: int = 0, part: int = 0) -> dict:
    streams_of = jax.random.split(jax.random.key(seed), 13)
    own_keys = jax.random.split(jax.random.fold_in(streams_of[12], part), 13)
    background = draw_background(jax.random.fold_in(jax.random.fold_in(streams_of[12], part), 71), part)
    decay_sq = jnp.clip(jnp.exp(math.log(0.5) - 3.218876 * jax.random.uniform(streams_of[1], (F, NLAT, NLON), jnp.float32) ** steps_of(streams_of[1], (F, NLAT, NLON), ((1, 4), (2, 4)), -0.2, 0.2)), 0.02, 0.5)
    edge_weight = jnp.clip(jnp.exp(math.log(1.0) - 2.3025851 * jax.random.uniform(streams_of[2], (DIRS, NLAT, NLON), jnp.float32) ** steps_of(streams_of[2], (DIRS, NLAT, NLON), ((1, 4), (2, 4)), -0.2, 0.2)), 0.1, 1.0)
    coupling = draw_coupling(jax.random.fold_in(streams_of[12], 71), part)
    obs_tiles = bell_draw(streams_of[4], (TILES, OBS, PATCH), PATCH ** -0.5, 0.375, ((0, 16),))
    obs_values = bell_draw(own_keys[5], (TILES, OBS), 3.0, 15.0, ((0, 16),), jnp.float32)
    obs_weights = jnp.clip(jnp.exp(math.log(32.0) - 2.0794415 * jax.random.uniform(streams_of[6], (TILES, OBS), jnp.float32) ** steps_of(streams_of[6], (TILES, OBS), ((0, 16),), -0.2, 0.2)), 4.0, 32.0)
    obs_counts = draw_obs_counts(jax.random.fold_in(streams_of[12], 71), part)
    swath_ids = with_ends(jax.random.randint(streams_of[8], (TILES,), 0, SWATHS), jax.random.fold_in(streams_of[8], 1), 0, SWATHS - 1).astype(jnp.int32)
    swath_scale = jnp.clip(jnp.exp(jax.random.uniform(streams_of[9], (SWATHS,), jnp.float32, math.log(0.5), math.log(2.0))), 0.5, 2.0)
    tile_owner = draw_tile_owner(jax.random.fold_in(streams_of[12], 71), part)
    tile_slot = with_ends(jax.random.randint(streams_of[11], (TILES,), 0, NPATCH_DEV), jax.random.fold_in(streams_of[11], 1), 0, NPATCH_DEV - 1).astype(jnp.int32)
    return {"background": background, "decay_sq": decay_sq, "edge_weight": edge_weight, "coupling": coupling, "obs_tiles": obs_tiles, "obs_values": obs_values, "obs_weights": obs_weights, "obs_counts": obs_counts, "swath_ids": swath_ids, "swath_scale": swath_scale, "tile_owner": tile_owner, "tile_slot": tile_slot}


DIRECTIONS = ((0, 1), (1, 0), (1, 1), (1, -1))


def stencil(padded, weights_pad, decay_part):
    rows_out = decay_part.shape[-2]
    cols_out = decay_part.shape[-1]

    def window_at(source, step_lat, step_lon):
        return source[..., 1 + step_lat:1 + step_lat + rows_out, 1 + step_lon:1 + step_lon + cols_out]

    center = window_at(padded, 0, 0)
    summed = decay_part * center
    for index_dir in range(4):
        step_lat, step_lon = DIRECTIONS[index_dir]
        weight_here = window_at(weights_pad[index_dir], 0, 0)
        weight_ahead = 0.5 * (weight_here + window_at(weights_pad[index_dir], step_lat, step_lon))
        weight_behind = 0.5 * (weight_here + window_at(weights_pad[index_dir], -step_lat, -step_lon))
        summed = summed + weight_ahead * (center - window_at(padded, step_lat, step_lon))
        summed = summed + weight_behind * (center - window_at(padded, -step_lat, -step_lon))
    return summed


def mix_fields(coupling, field_in):
    return jnp.einsum("fg,gyx->fyx", coupling, field_in, precision=lax.Precision.HIGHEST)


def pad_grid(field_in, pad_depth):
    wrapped = jnp.concatenate([field_in[..., -pad_depth:], field_in, field_in[..., :pad_depth]], axis=-1)
    return jnp.pad(wrapped, ((0, 0), (pad_depth, pad_depth), (0, 0)))


def reference(background, decay_sq, edge_weight, coupling, obs_tiles, obs_values, obs_weights, obs_counts, swath_ids, swath_scale, tile_owner, tile_slot):
    weights_pad = pad_grid(edge_weight, 1)

    def prior_apply(field_in):
        first_pass = stencil(pad_grid(field_in, 1), weights_pad, decay_sq)
        return stencil(pad_grid(mix_fields(coupling, first_pass), 1), weights_pad, decay_sq)

    tile_index = jnp.arange(TILES).astype(jnp.int32)
    block_row = (tile_index // TILE_DEV) % ROW_DEVS
    per_field = CLAT * CLON // PATCH
    per_row = CLON // PATCH
    field_of = tile_slot // per_field
    lat_of = block_row * CLAT + (tile_slot % per_field) // per_row
    lon_of = tile_owner * per_row + tile_slot % per_row

    lookup = jnp.sum(jnp.where(swath_ids[:, None] == jnp.arange(SWATHS)[None, :], swath_scale[None, :], 0.0), axis=1)
    live_rows = jnp.arange(OBS)[None, :] < obs_counts[:, None]
    weight_eff = jnp.where(live_rows, obs_weights * lookup[:, None], 0.0)

    tiles_grouped = obs_tiles.reshape(TILES // TILE_DEV, TILE_DEV, OBS, PATCH)

    def tiles_forward(inputs):
        def one_block(block_pair):
            block_tiles, block_inputs = block_pair
            return jnp.einsum("top,tp->to", block_tiles.astype(jnp.float32), block_inputs.astype(jnp.float32))
        return lax.map(one_block, (tiles_grouped, inputs.reshape(-1, TILE_DEV, PATCH))).reshape(TILES, OBS)

    def tiles_adjoint(weighted):
        def one_block(block_pair):
            block_tiles, block_weighted = block_pair
            return jnp.einsum("top,to->tp", block_tiles.astype(jnp.float32), block_weighted.astype(jnp.float32))
        return lax.map(one_block, (tiles_grouped, weighted.reshape(-1, TILE_DEV, OBS))).reshape(TILES, PATCH)

    def place(contribution):
        grid_view = jnp.zeros((F, NLAT, NLON // PATCH, PATCH), jnp.float32)
        grid_view = grid_view.at[field_of, lat_of, lon_of].add(contribution)
        return grid_view.reshape(F, NLAT, NLON)

    def obs_apply(field_in):
        inputs = field_in.reshape(F, NLAT, NLON // PATCH, PATCH)[field_of, lat_of, lon_of].astype(jnp.bfloat16)
        applied = tiles_forward(inputs)
        weighted = (weight_eff * applied).astype(jnp.bfloat16)
        return place(tiles_adjoint(weighted))

    def operate(field_in):
        return prior_apply(field_in) + obs_apply(field_in)

    scaled_obs = (weight_eff * obs_values).astype(jnp.bfloat16)
    right_side = prior_apply(background) + place(tiles_adjoint(scaled_obs))

    solution = jnp.zeros_like(right_side)
    residual = right_side
    direction = right_side
    norm_now = jnp.sum(residual * residual)
    for iteration in range(ITERS):
        applied = operate(direction)
        step_size = norm_now / jnp.sum(direction * applied)
        solution = solution + step_size * direction
        residual = residual - step_size * applied
        norm_next = jnp.sum(residual * residual)
        direction = residual + (norm_next / norm_now) * direction
        norm_now = norm_next
    return solution, residual
```

```python
import functools

import jax
import jax.numpy as jnp
from jax import lax
from jax.experimental import pallas as pl
from jax.experimental.pallas import tpu as pltpu
from jax.sharding import PartitionSpec as P

CAP = 4
ITERS = 3
SLOT_ROWS = 8
EDGE = 128
FIRST_GRAMS = 6
MESH = pl.DeviceIdType.MESH


def loop(low, high, body):
    if high - low <= 16:
        for k in range(low, high):
            body(k)
    else:
        lax.fori_loop(low, high, lambda k, c: (body(k), c)[1], 0)


def kernel(
    sizes,
    owner_hbm,
    slot_hbm,
    counts_hbm,
    swath_hbm,
    scale_hbm,
    coupling_hbm,
    bg_hbm,
    decay_hbm,
    edge_hbm,
    tiles_hbm,
    values_hbm,
    weights_hbm,
    sol_out,
    res_out,
    owner_s,
    slot_s,
    counts_s,
    swath_s,
    scale_s,
    coupling_s,
    bg,
    decay,
    edge,
    obs_values,
    obs_weights,
    tiles,
    gram,
    w_parts,
    q_rows,
    tile_of,
    coef,
    coef_m,
    diag,
    diag_m,
    vec,
    vec_m,
    old,
    old_m,
    pdir,
    qs,
    qm,
    raw_m,
    pk_out,
    pk_in,
    pkm_in,
    ask,
    req,
    ask_row,
    req_row,
    gather_oh,
    own_oh,
    rim_oh,
    xs,
    xr,
    yv,
    yr,
    msg,
    msg_in,
    part,
    parts,
    halo_send,
    halo_recv,
    ask_send,
    ask_recv,
    x_send,
    x_recv,
    y_send,
    y_recv,
    m_send,
    m_recv,
    red_send,
    red_recv,
    load_sem,
):
    lon_n, lat_n, fld_n = sizes
    row_n = lat_n * fld_n
    dev_n = lon_n * row_n
    fields, rows, cols = bg.shape
    tile_n, obs_len, patch = tiles.shape
    ext = cols + 2 * EDGE
    per_row = cols // patch
    patch_n = fields * rows * per_row
    pos_n = lon_n * SLOT_ROWS
    bf16, f32, i32 = jnp.bfloat16, jnp.float32, jnp.int32

    my_lon = lax.axis_index("lon")
    my_row = lax.axis_index("lat") * fld_n + lax.axis_index("fld")
    me = my_lon * row_n + my_row

    def device(lon, row):
        return {"lon": lon, "lat": row // fld_n, "fld": row % fld_n}

    west, east = (my_lon + lon_n - 1) % lon_n, (my_lon + 1) % lon_n
    north, south = (my_row + row_n - 1) % row_n, (my_row + 1) % row_n
    has_north = my_row > 0
    has_south = my_row < row_n - 1

    loads = [
        pltpu.make_async_copy(src, dst, load_sem.at[k])
        for k, (src, dst) in enumerate(
            (
                (owner_hbm, owner_s),
                (slot_hbm, slot_s),
                (counts_hbm, counts_s),
                (swath_hbm, swath_s),
                (scale_hbm, scale_s),
                (coupling_hbm, coupling_s),
                (values_hbm, obs_values),
                (weights_hbm, obs_weights),
                (edge_hbm, edge),
                (bg_hbm, bg),
                (decay_hbm, decay),
                (tiles_hbm, tiles),
            )
        )
    ]
    for load in loads:
        load.start()

    barrier = pltpu.get_barrier_semaphore()

    def greet(k):
        other = (me + k) % dev_n
        pl.semaphore_signal(
            barrier, inc=1, device_id=device(other // row_n, other % row_n), device_id_type=MESH
        )

    loop(1, dev_n, greet)

    center = slice(EDGE, EDGE + cols)
    lane8 = lax.broadcasted_iota(i32, (rows, EDGE), 1)
    sub_e = lax.broadcasted_iota(i32, (rows, ext), 0)
    top, bottom = sub_e == 0, sub_e == rows - 1
    rim_mask = ((sub_e < 2) & has_south) | ((sub_e >= rows - 2) & has_north)

    def remote(src, dst, send_sem, recv_sem, lon, row):
        return pltpu.make_async_remote_copy(
            src_ref=src,
            dst_ref=dst,
            send_sem=send_sem,
            recv_sem=recv_sem,
            device_id=device(lon, row),
            device_id_type=MESH,
        )

    def wait_bytes(some, sem):
        pltpu.make_async_copy(some, some, sem).wait()

    def turn(value, by):
        return pltpu.roll(value, by % EDGE, 1) if by % EDGE else value

    first_two, last_two = pl.ds(0, 2), pl.ds(rows - 2, 2)

    def halo_copies(h):
        pairs = [
            (pk_out.at[h, 0], pk_in.at[h, 1], west, my_row),
            (pk_out.at[h, 1], pk_in.at[h, 0], east, my_row),
            (pk_out.at[h, 0, first_two], pkm_in.at[h, 1, first_two], west, north),
            (pk_out.at[h, 1, first_two], pkm_in.at[h, 0, first_two], east, north),
            (pk_out.at[h, 0, last_two], pkm_in.at[h, 1, last_two], west, south),
            (pk_out.at[h, 1, last_two], pkm_in.at[h, 0, last_two], east, south),
        ]
        if h == 0:
            bands = [(bg, raw_m.at[0]), (edge, raw_m.at[1]), (decay, raw_m.at[2])]
        else:
            bands = [(qs.at[h - 1], qm.at[h - 1])]
        for src, dst in bands:
            pairs.append((src.at[:, first_two], dst.at[:, first_two], my_lon, north))
            pairs.append((src.at[:, last_two], dst.at[:, last_two], my_lon, south))
        return [
            remote(src, dst, halo_send.at[h, k], halo_recv.at[h, k], lon, row)
            for k, (src, dst, lon, row) in enumerate(pairs)
        ]

    def pack(h, values):
        to_west = jnp.zeros((rows, EDGE), f32)
        to_east = to_west
        for g, value in enumerate(values):
            here = lane8 // 2 == g
            to_west = jnp.where(here, turn(value[:, 0:EDGE], 2 * g), to_west)
            to_east = jnp.where(here, turn(value[:, cols - EDGE : cols], 2 * g + 2), to_east)
        pk_out[h, 0] = to_west
        pk_out[h, 1] = to_east

    def west_part(buffer, h, g):
        return turn(buffer[h, 0], EDGE - 2 - 2 * g)

    def east_part(buffer, h, g):
        return turn(buffer[h, 1], EDGE - 2 * g)

    def widened(value, h, g):
        return jnp.concatenate([west_part(pk_in, h, g), value, east_part(pk_in, h, g)], axis=1)

    def widened_m(value, h, g):
        wide = jnp.concatenate([west_part(pkm_in, h, g), value, east_part(pkm_in, h, g)], axis=1)
        return jnp.where(rim_mask, wide, 0.0)

    def y_put(i, value):
        pos_half = lax.broadcasted_iota(i32, (pos_n, patch), 0) % SLOT_ROWS < CAP
        high = value.astype(bf16).astype(f32)
        both = jnp.where(pos_half, high, value - high)
        full = both.astype(bf16)
        yv[i] = full
        yr[i, my_lon] = full
        if i < ITERS:
            blocks = [both[l * SLOT_ROWS : (l + 1) * SLOT_ROWS] for l in range(lon_n)]
            for l in range(lon_n):
                rim = jnp.concatenate(
                    [blocks[l - 1][:, patch - EDGE :], blocks[(l + 1) % lon_n][:, :EDGE]], axis=1
                )
                msg[i, l] = jnp.concatenate([blocks[l], rim], axis=0).astype(bf16)

    def y_start(i):
        def send(k):
            remote(
                yv.at[i], yr.at[i, my_lon], y_send.at[i], y_recv.at[i], (my_lon + k) % lon_n, my_row
            ).start()

        loop(1, lon_n, send)
        if i < ITERS:

            def send_rim(k):
                to = (my_lon + k) % lon_n
                remote(
                    msg.at[i, to], msg_in.at[i, 1, my_lon], m_send.at[i], m_recv.at[i], to, north
                ).start()
                remote(
                    msg.at[i, to], msg_in.at[i, 0, my_lon], m_send.at[i], m_recv.at[i], to, south
                ).start()

            loop(0, lon_n, send_rim)

    def x_start(i):
        def send(k):
            to = (my_lon + k) % lon_n
            remote(
                xs.at[i, to, pl.ds(0, CAP)],
                xr.at[i, my_lon, pl.ds(0, CAP)],
                x_send.at[i],
                x_recv.at[i],
                to,
                my_row,
            ).start()

        loop(1, lon_n, send)

    def x_wait(sem, i):
        wait_bytes(xr.at[i, pl.ds(0, lon_n - 1), pl.ds(0, CAP)], sem.at[i])

    def y_wait(sem, i):
        wait_bytes(yr.at[i, pl.ds(0, lon_n - 1)], sem.at[i])

    def m_wait(sem, i):
        wait_bytes(msg_in.at[i], sem.at[i])

    def total_start(k, value):
        part[k] = value
        parts[k, me] = value

        def send(j):
            other = (me + j) % dev_n
            remote(
                part.at[k],
                parts.at[k, me],
                red_send.at[k],
                red_recv.at[k],
                other // row_n,
                other % row_n,
            ).start()

        loop(1, dev_n, send)

    def total_wait(sem, k):
        wait_bytes(parts.at[k, pl.ds(0, dev_n - 1)], sem.at[k])

    def lanes_of(value):
        lane_sum = value[:, 0:128]
        for k in range(1, value.shape[1] // 128):
            lane_sum = lane_sum + value[:, k * 128 : (k + 1) * 128]
        return jnp.sum(lane_sum, axis=0, keepdims=True)

    def mixed(values, f):
        acc = coupling_s[f, 0] * values[0]
        for g in range(1, fields):
            acc = acc + coupling_s[f, g] * values[g]
        return acc

    for load in loads[:8]:
        load.wait()

    pos_row = lax.broadcasted_iota(i32, (pos_n, 128), 0)
    row_lane = lax.broadcasted_iota(i32, (8, 128), 1)
    tile_row = lax.broadcasted_iota(i32, (tile_n, obs_len), 0)
    obs_lane = lax.broadcasted_iota(i32, (tile_n, obs_len), 1)
    holds = jnp.full((pos_n, 128), -1, i32)
    asked = jnp.full((pos_n, 128), -2, i32)
    asked_row = jnp.full((8, 128), -1, i32)
    scale_of = jnp.zeros((tile_n, obs_len), f32)
    count_of = jnp.zeros((tile_n, obs_len), i32)
    for t in range(tile_n):
        rank = jnp.int32(0)
        for other in range(t):
            rank = rank + (owner_s[other] == owner_s[t]).astype(i32)
        number = slot_s[t]
        column, rest = number % per_row, number // per_row
        moved = (column * fields + rest // rows) * rows + rest % rows
        place = owner_s[t] * SLOT_ROWS + rank
        here = (pos_row == place) | (pos_row == place + CAP)
        here_row = (row_lane == place) | (row_lane == place + CAP)
        holds = jnp.where(here, t, holds)
        asked = jnp.where(here, moved, asked)
        asked_row = jnp.where(here_row, moved, asked_row)
        scale_of = jnp.where(tile_row == t, scale_s[swath_s[t]], scale_of)
        count_of = jnp.where(tile_row == t, counts_s[t], count_of)
    tile_of[...] = jnp.concatenate([holds] * (patch // 128), axis=1)
    ask[...] = asked.reshape(lon_n, SLOT_ROWS, 128)
    req[my_lon] = ask[my_lon]
    ask_row[...] = asked_row[0:1]
    req_row[lon_n + my_lon] = asked_row[0:1]
    weight = jnp.where(obs_lane < count_of, obs_weights[...] * scale_of, 0.0)
    weight_high = weight.astype(bf16).astype(f32)
    w_parts[...] = jnp.concatenate([weight_high, weight - weight_high], axis=0).astype(bf16)
    q_rows[...] = (weight * obs_values[...]).astype(bf16).astype(f32)

    for load in loads[8:11]:
        load.wait()
    pack(0, [bg[f] for f in range(fields)] + [edge[e] for e in range(4)] + [decay[f] for f in range(fields)])

    pl.semaphore_wait(barrier, dev_n - 1)
    for copy in halo_copies(0):
        copy.start()

    def send_ask(k):
        to = (my_lon + k) % lon_n
        remote(ask.at[to], req.at[my_lon], ask_send.at[0], ask_recv.at[0], to, my_row).start()
        remote(
            ask_row, req_row.at[lon_n + my_lon], ask_send.at[1], ask_recv.at[1], to, my_row
        ).start()

    def send_ask_rim(k):
        to = (my_lon + k) % lon_n
        remote(
            ask_row, req_row.at[2 * lon_n + my_lon], ask_send.at[1], ask_recv.at[1], to, north
        ).start()
        remote(ask_row, req_row.at[my_lon], ask_send.at[1], ask_recv.at[1], to, south).start()

    loop(1, lon_n, send_ask)
    loop(0, lon_n, send_ask_rim)

    def spread(value, t):
        return jnp.where(tile_of[...] == t, value, 0.0).astype(bf16)

    loads[11].wait()
    acc = None
    for t in range(tile_n):
        term = jnp.dot(
            spread(q_rows[t : t + 1, :], t), tiles[t], preferred_element_type=f32
        )
        acc = term if acc is None else acc + term
    y_put(0, acc)
    y_start(0)

    pick_row = lax.broadcasted_iota(i32, (2 * tile_n, 128), 0) % tile_n

    def gram_of(t, carry):
        chosen = jnp.where(pick_row == t, 1.0, 0.0).astype(bf16)
        column = lax.dot_general(
            w_parts[...], chosen, (((0,), (0,)), ((), ())), preferred_element_type=f32
        )
        tile = tiles[t]
        scaled = (tile.astype(f32) * jnp.concatenate([column] * (patch // 128), axis=1)).astype(bf16)
        gram[t] = lax.dot_general(
            tile, scaled, (((0,), (0,)), ((), ())), preferred_element_type=f32
        ).astype(bf16)
        return carry

    lax.fori_loop(0, FIRST_GRAMS, gram_of, 0)

    for copy in halo_copies(0):
        copy.wait_recv()
    w = [widened(edge[e], 0, 4 + e) for e in range(4)]
    wm = [widened_m(raw_m[1, e], 0, 4 + e) for e in range(4)]

    def around(main, rim):
        m1, r1 = pltpu.roll(main, 1, 0), pltpu.roll(rim, 1, 0)
        m7, r7 = pltpu.roll(main, rows - 1, 0), pltpu.roll(rim, rows - 1, 0)
        return (
            jnp.where(top, r1, m1),
            jnp.where(bottom, r7, m7),
            jnp.where(top, m1, r1),
            jnp.where(bottom, m7, r7),
        )

    near = [around(w[e], wm[e]) for e in range(4)]

    def coefficients(here, up, down, coef_ref, diag_ref, decays):
        w_west = {e: pltpu.roll(here[e], 1, 1) for e in (0, 2, 3)}
        w_east = {e: pltpu.roll(here[e], ext - 1, 1) for e in (0, 2, 3)}
        e0, e1, e2 = (
            0.5 * (w_west[0] + here[0]),
            0.5 * (w_west[3] + up[3]),
            0.5 * (w_west[2] + down[2]),
        )
        v0, v1, v2 = (
            0.5 * (w_east[0] + here[0]),
            0.5 * (w_east[2] + up[2]),
            0.5 * (w_east[3] + down[3]),
        )
        n0, n1 = 0.5 * (here[1] + up[1]), 0.5 * (here[1] + down[1])
        for k, value in enumerate((e0, e1, e2, v0, v1, v2, n0, n1)):
            coef_ref[k] = value
        degree = (
            n0 + n1 + pltpu.roll(e0 + e1 + e2, ext - 1, 1) + pltpu.roll(v0 + v1 + v2, 1, 1)
        )
        for f in range(fields):
            diag_ref[f] = decays[f] + degree

    coefficients(
        w,
        [near[e][0] for e in range(4)],
        [near[e][1] for e in range(4)],
        coef,
        diag,
        [widened(decay[f], 0, 8 + f) for f in range(fields)],
    )
    coefficients(
        wm,
        [near[e][2] for e in range(4)],
        [near[e][3] for e in range(4)],
        coef_m,
        diag_m,
        [widened_m(raw_m[2, f], 0, 8 + f) for f in range(fields)],
    )

    def apply_l(c, d, value, up, down):
        toward_east = c[0] * value + c[1] * up + c[2] * down
        toward_west = c[3] * value + c[4] * up + c[5] * down
        result = d * value - c[6] * up - c[7] * down
        return result - pltpu.roll(toward_east, ext - 1, 1) - pltpu.roll(toward_west, 1, 1)

    def first_pass(main, rim):
        out, out_m = [], []
        for f in range(fields):
            up, down, up_m, down_m = around(main[f], rim[f])
            out.append(apply_l(coef, diag[f], main[f], up, down))
            out_m.append(apply_l(coef_m, diag_m[f], rim[f], up_m, down_m))
        return out, out_m

    def second_pass(h, first, first_m):
        u = [mixed(first, f) for f in range(fields)]
        um = [jnp.where(rim_mask, mixed(first_m, f), 0.0) for f in range(fields)]
        for f in range(fields):
            up, down, _, _ = around(u[f], um[f])
            qs[h, f] = apply_l(coef, diag[f], u[f], up, down)[:, center]
        return u

    def send_q(h):
        pack(h + 1, [qs[h, f] for f in range(fields)])
        for copy in halo_copies(h + 1):
            copy.start()
        stacked = jnp.concatenate(
            [
                qs[h, f, :, c * patch : (c + 1) * patch]
                for c in range(per_row)
                for f in range(fields)
            ],
            axis=0,
        )
        high = stacked.astype(bf16)
        low = (stacked - high.astype(f32)).astype(bf16)
        chosen = gather_oh[...]
        patches = jnp.dot(chosen, low, preferred_element_type=f32) + jnp.dot(
            chosen, high, preferred_element_type=f32
        )
        xs[h] = patches.reshape(lon_n, SLOT_ROWS, patch)
        x_start(h)
        xr[h, my_lon] = xs[h, my_lon]

    main = [widened(bg[f], 0, f) for f in range(fields)]
    rim = [widened_m(raw_m[0, f], 0, f) for f in range(fields)]
    first, first_m = first_pass(main, rim)
    second_pass(0, first, first_m)

    wait_bytes(req.at[pl.ds(0, lon_n - 1)], ask_recv.at[0])
    wanted = req[...].reshape(pos_n, 128)
    wanted = jnp.concatenate([wanted] * (patch_n // 128), axis=1)
    picked = wanted == lax.broadcasted_iota(i32, (pos_n, patch_n), 1)
    gather_oh[...] = jnp.where(picked, 1.0, 0.0).astype(bf16)
    send_q(0)

    wait_bytes(req_row.at[pl.ds(0, 3 * lon_n - 1)], ask_recv.at[1])
    lane1 = lax.broadcasted_iota(i32, (1, 128), 1)
    own_k, rim_k = lon_n * pos_n, 2 * lon_n * 2 * SLOT_ROWS

    def iota(n, axis):
        return lax.broadcasted_iota(i32, (n, 128), axis)

    own_rows = iota(patch_n, 0)
    side_rows = iota(fields * rows, 0)
    for group in range(own_k // 128):
        slots = jnp.full((1, 128), -1, i32)
        for h in range(lon_n):
            if h * pos_n // 128 == group:
                offset = h * pos_n % 128
                moved = turn(req_row[lon_n + h], offset)
                slots = jnp.where((lane1 >= offset) & (lane1 < offset + pos_n), moved, slots)
        lanes = slice(group * 128, (group + 1) * 128)
        at = lane1 % pos_n // SLOT_ROWS

        def match(rows_of, owner):
            wanted = jnp.where(at == owner, slots, -1)
            return jnp.where(rows_of == wanted, 1.0, 0.0).astype(bf16)

        own_oh[0:patch_n, lanes] = match(own_rows, my_lon)
        first_side, last_side = patch_n, patch_n + fields * rows
        own_oh[first_side:last_side, lanes] = match(
            (per_row - 1) * fields * rows + side_rows, west
        )
        own_oh[last_side : last_side + fields * rows, lanes] = match(side_rows, east)
        tile_rows = last_side + fields * rows
        mine = (iota(pos_n, 0) // SLOT_ROWS == at) & (ask[...].reshape(pos_n, 128) == slots)
        own_oh[tile_rows : tile_rows + pos_n, lanes] = jnp.where(mine, 1.0, 0.0).astype(bf16)

    for group in range(rim_k // 128):
        ours = jnp.full((1, 128), -1, i32)
        from_west, from_east = ours, ours
        side = group * 128 // (rim_k // 2)
        for index in range(2 * lon_n):
            if index * 2 * SLOT_ROWS // 128 != group:
                continue
            offset = index * 2 * SLOT_ROWS % 128
            table = jnp.broadcast_to(
                req_row[(index // lon_n) * 2 * lon_n + index % lon_n], (8, 128)
            )
            low = (lane1 >= offset) & (lane1 < offset + SLOT_ROWS)
            high = (lane1 >= offset + SLOT_ROWS) & (lane1 < offset + 2 * SLOT_ROWS)

            def brought(owner, to):
                by = (to - owner * SLOT_ROWS + 2 * 128) % 128
                return pltpu.roll(table, by, 1)[0:1]

            ours = jnp.where(low, brought(my_lon, offset), ours)
            from_west = jnp.where(high, brought(west, offset + SLOT_ROWS), from_west)
            from_east = jnp.where(high, brought(east, offset + SLOT_ROWS), from_east)
        lanes = slice(group * 128, (group + 1) * 128)
        is_north = (group * 128 + lane1) < rim_k // 2

        def match_rim(row_ids, wanted):
            sub = row_ids % rows
            keep = (is_north & has_north & (sub >= rows - 2)) | (
                (~is_north) & has_south & (sub < 2)
            )
            return jnp.where(keep & (row_ids == wanted), 1.0, 0.0).astype(bf16)

        rim_oh[0:patch_n, lanes] = match_rim(own_rows, ours)
        rim_oh[patch_n : patch_n + fields * rows, lanes] = match_rim(
            (per_row - 1) * fields * rows + side_rows, from_west
        )
        rim_oh[patch_n + fields * rows :, lanes] = match_rim(side_rows, from_east)

    lax.fori_loop(FIRST_GRAMS, tile_n, gram_of, 0)

    pos_sub = lax.broadcasted_iota(i32, (pos_n, patch), 0) % SLOT_ROWS

    def placed_field(blocks, f):
        return jnp.concatenate(
            [
                blocks[(c * fields + f) * rows : (c * fields + f + 1) * rows]
                for c in range(per_row)
            ],
            axis=1,
        )

    def received(h, i):
        x_wait(x_recv, h)
        y_wait(y_recv, i)
        blocks = jnp.dot(
            own_oh[...], yr[i].reshape(own_k, patch), preferred_element_type=f32
        )
        came = xr[h].reshape(pos_n, patch)
        came = jnp.where(pos_sub < CAP, came, pltpu.roll(came, CAP, 0))
        seen = came + blocks[patch_n + 2 * fields * rows :]
        return seen, blocks

    def assembled(h, i, blocks):
        for copy in halo_copies(h + 1):
            copy.wait_recv()
        m_wait(m_recv, i)
        rim_blocks = jnp.dot(
            rim_oh[...], msg_in[i].reshape(rim_k, patch), preferred_element_type=f32
        )
        main, rim = [], []
        for f in range(fields):
            west_rows = slice(patch_n + f * rows, patch_n + (f + 1) * rows)
            east_rows = slice(patch_n + (fields + f) * rows, patch_n + (fields + f + 1) * rows)
            main.append(
                jnp.concatenate(
                    [
                        west_part(pk_in, h + 1, f) + blocks[west_rows, patch - EDGE :],
                        qs[h, f] + placed_field(blocks, f),
                        east_part(pk_in, h + 1, f) + blocks[east_rows, :EDGE],
                    ],
                    axis=1,
                )
            )
            rim.append(
                widened_m(qm[h, f], h + 1, f)
                + jnp.concatenate(
                    [
                        rim_blocks[west_rows, :EDGE],
                        placed_field(rim_blocks, f),
                        rim_blocks[east_rows, patch - EDGE :],
                    ],
                    axis=1,
                )
            )
        return main, rim

    def tile_images(seen):
        acc = None
        for t in range(tile_n):
            term = jnp.dot(spread(seen, t), gram[t], preferred_element_type=f32)
            acc = term if acc is None else acc + term
        return acc

    seen, blocks = received(0, 0)
    x_old = None
    gamma_old = alpha = beta = None
    for it in range(ITERS):
        last = it == ITERS - 1
        images = tile_images(seen)
        y_put(it + 1, images)
        y_start(it + 1)
        if it == 0:
            main, rim = assembled(0, 0, blocks)
            for f in range(fields):
                vec[f], vec_m[f] = main[f], rim[f]
        else:
            image, image_m = assembled(it, it, blocks)
            for f in range(fields):
                step_vec = image[f] if it == 1 else image[f] + beta * old[f]
                step_m = image_m[f] if it == 1 else image_m[f] + beta * old_m[f]
                old[f], old_m[f] = step_vec, step_m
                here = vec[f, :, center]
                p_new = here if it == 1 else here + beta * pdir[f]
                pdir[f] = p_new
                sol_out[f] = alpha * p_new if it == 1 else sol_out[f] + alpha * p_new
                vec[f] = vec[f] - alpha * step_vec
                vec_m[f] = vec_m[f] - alpha * step_m
        main = [vec[f] for f in range(fields)]
        rim = [vec_m[f] for f in range(fields)]
        first, first_m = first_pass(main, rim)
        u = [mixed(first, f)[:, center] for f in range(fields)]
        gamma_part = jnp.zeros((1, 128), f32)
        delta_part = lanes_of(jnp.where(pos_sub < CAP, seen * images, 0.0))
        for f in range(fields):
            here = main[f][:, center]
            gamma_part = gamma_part + lanes_of(here * here)
            delta_part = delta_part + lanes_of(u[f] * first[f][:, center])
        total_start(it, jnp.concatenate([gamma_part, delta_part], axis=1))
        second_pass(it + 1, first, first_m)
        if not last:
            send_q(it + 1)
            new_seen, blocks = received(it + 1, it + 1)
        else:
            y_wait(y_recv, it + 1)
            blocks = jnp.dot(
                own_oh[0:patch_n, :], yr[it + 1].reshape(own_k, patch), preferred_element_type=f32
            )
        total_wait(red_recv, it)
        sums = jnp.sum(parts[it], axis=0)
        gamma = jnp.sum(sums[:, 0:128], axis=1, keepdims=True)
        delta = jnp.sum(sums[:, 128:256], axis=1, keepdims=True)
        if it == 0:
            alpha = gamma / delta
        else:
            beta = gamma / gamma_old
            alpha = gamma / (delta - beta * gamma / alpha)
        gamma_old = gamma
        if not last:
            x_step = new_seen if it == 0 else new_seen + beta * x_old
            x_old = x_step
            seen = seen - alpha * x_step
        else:
            for f in range(fields):
                image = qs[it + 1, f] + placed_field(blocks, f)
                here = vec[f, :, center]
                step_vec = image + beta * old[f, :, center]
                sol_out[f] = sol_out[f] + alpha * (here + beta * pdir[f])
                res_out[f] = here - alpha * step_vec

    for h in range(ITERS + 1):
        for copy in halo_copies(h):
            copy.wait_send()
    wait_bytes(req.at[pl.ds(0, lon_n - 1)], ask_send.at[0])
    wait_bytes(req_row.at[pl.ds(0, 3 * lon_n - 1)], ask_send.at[1])
    for i in range(ITERS + 1):
        y_wait(y_send, i)
    for i in range(ITERS):
        x_wait(x_send, i)
        m_wait(m_send, i)
        total_wait(red_send, i)


def on_device(
    sizes,
    background,
    decay_sq,
    edge_weight,
    coupling,
    obs_tiles,
    obs_values,
    obs_weights,
    obs_counts,
    swath_ids,
    swath_scale,
    tile_owner,
    tile_slot,
):
    fields, rows, cols = background.shape
    tile_n, obs_len, patch = obs_tiles.shape
    lon_n, lat_n, fld_n = sizes
    dev_n = lon_n * lat_n * fld_n
    ext = cols + 2 * EDGE
    pos_n = lon_n * SLOT_ROWS
    patch_n = fields * rows * cols // patch
    side_n = 2 * fields * rows
    halos = ITERS + 1
    f32, bf16, i32 = jnp.float32, jnp.bfloat16, jnp.int32
    vmem = pl.BlockSpec(memory_space=pltpu.VMEM)
    dma = pltpu.SemaphoreType.DMA
    shape = pltpu.VMEM((fields, rows, cols), f32)
    block = pltpu.VMEM((fields, rows, ext), f32)
    return pl.pallas_call(
        functools.partial(kernel, sizes),
        out_shape=(shape, shape),
        in_specs=[pl.BlockSpec(memory_space=pltpu.HBM)] * 12,
        out_specs=(vmem, vmem),
        scratch_shapes=[
            pltpu.SMEM(tile_owner.shape, i32),
            pltpu.SMEM(tile_slot.shape, i32),
            pltpu.SMEM(obs_counts.shape, i32),
            pltpu.SMEM(swath_ids.shape, i32),
            pltpu.SMEM(swath_scale.shape, f32),
            pltpu.SMEM(coupling.shape, f32),
            pltpu.VMEM(background.shape, f32),
            pltpu.VMEM(decay_sq.shape, f32),
            pltpu.VMEM(edge_weight.shape, f32),
            pltpu.VMEM(obs_values.shape, f32),
            pltpu.VMEM(obs_weights.shape, f32),
            pltpu.VMEM((tile_n, obs_len, patch), bf16),
            pltpu.VMEM((tile_n, patch, patch), bf16),
            pltpu.VMEM((2 * tile_n, obs_len), bf16),
            pltpu.VMEM((tile_n, obs_len), f32),
            pltpu.VMEM((pos_n, patch), i32),
            pltpu.VMEM((8, rows, ext), f32),
            pltpu.VMEM((8, rows, ext), f32),
            block,
            block,
            block,
            block,
            block,
            block,
            pltpu.VMEM((fields, rows, cols), f32),
            pltpu.VMEM((ITERS + 1, fields, rows, cols), f32),
            pltpu.VMEM((ITERS, fields, rows, cols), f32),
            pltpu.VMEM((3, fields, rows, cols), f32),
            pltpu.VMEM((halos, 2, rows, EDGE), f32),
            pltpu.VMEM((halos, 2, rows, EDGE), f32),
            pltpu.VMEM((halos, 2, rows, EDGE), f32),
            pltpu.VMEM((lon_n, SLOT_ROWS, 128), i32),
            pltpu.VMEM((lon_n, SLOT_ROWS, 128), i32),
            pltpu.VMEM((1, 128), i32),
            pltpu.VMEM((3 * lon_n, 1, 128), i32),
            pltpu.VMEM((pos_n, patch_n), bf16),
            pltpu.VMEM((patch_n + side_n + pos_n, lon_n * pos_n), bf16),
            pltpu.VMEM((patch_n + side_n, 4 * lon_n * SLOT_ROWS), bf16),
            pltpu.VMEM((ITERS, lon_n, SLOT_ROWS, patch), f32),
            pltpu.VMEM((ITERS, lon_n, SLOT_ROWS, patch), f32),
            pltpu.VMEM((ITERS + 1, pos_n, patch), bf16),
            pltpu.VMEM((ITERS + 1, lon_n, pos_n, patch), bf16),
            pltpu.VMEM((ITERS, lon_n, 2 * SLOT_ROWS, patch), bf16),
            pltpu.VMEM((ITERS, 2, lon_n, 2 * SLOT_ROWS, patch), bf16),
            pltpu.VMEM((ITERS, 1, 256), f32),
            pltpu.VMEM((ITERS, dev_n, 1, 256), f32),
            dma((halos, 12)),
            dma((halos, 12)),
            dma((2,)),
            dma((2,)),
            dma((ITERS,)),
            dma((ITERS,)),
            dma((ITERS + 1,)),
            dma((ITERS + 1,)),
            dma((ITERS,)),
            dma((ITERS,)),
            dma((ITERS,)),
            dma((ITERS,)),
            dma((12,)),
        ],
        compiler_params=pltpu.CompilerParams(
            collective_id=0, has_side_effects=True, vmem_limit_bytes=67043328 - 3 * 2**20
        ),
    )(
        tile_owner,
        tile_slot,
        obs_counts,
        swath_ids,
        swath_scale,
        coupling,
        background,
        decay_sq,
        edge_weight,
        obs_tiles,
        obs_values,
        obs_weights,
    )


def solution(mesh):
    sizes = (mesh.shape["lon"], mesh.shape["lat"], mesh.shape["fld"])
    return jax.shard_map(
        functools.partial(on_device, sizes),
        mesh=mesh,
        in_specs=(
            P("group", ("lat", "fld"), "lon"),
            P(None, ("lat", "fld"), "lon"),
            P(None, ("lat", "fld"), "lon"),
            P(),
            P(("lon", "lat", "fld"), None, None),
            P(("group", "lon", "lat", "fld"), None),
            P(("lon", "lat", "fld"), None),
            P(("lon", "lat", "fld")),
            P(("lon", "lat", "fld")),
            P(),
            P(("lon", "lat", "fld")),
            P(("lon", "lat", "fld")),
        ),
        out_specs=(P("group", ("lat", "fld"), "lon"), P("group", ("lat", "fld"), "lon")),
        check_vma=False,
    )
```

```python
import functools

import jax
import jax.numpy as jnp
from jax import lax
from jax.experimental import pallas as pl
from jax.experimental.pallas import tpu as pltpu
from jax.sharding import PartitionSpec as P

CAP = 4
ITERS = 3
SLOT_ROWS = 8
EDGE = 128
GRAMS_AHEAD = 5
GRAMS_NEXT = 13
MESH = pl.DeviceIdType.MESH


def loop(low, high, body):
    if high - low <= 16:
        for k in range(low, high):
            body(k)
    else:
        lax.fori_loop(low, high, lambda k, c: (body(k), c)[1], 0)


def kernel(
    sizes,
    owner_hbm,
    slot_hbm,
    counts_hbm,
    swath_hbm,
    scale_hbm,
    coupling_hbm,
    bg_hbm,
    decay_hbm,
    edge_hbm,
    tiles_hbm,
    values_hbm,
    weights_hbm,
    sol_out,
    res_out,
    owner_s,
    slot_s,
    counts_s,
    swath_s,
    scale_s,
    coupling_s,
    bg,
    decay,
    edge,
    obs_values,
    obs_weights,
    tiles,
    gram,
    w_parts,
    q_rows,
    tile_of,
    coef,
    coef_m,
    diag,
    diag_m,
    vecs,
    vec_m,
    qs,
    qm,
    raw_m,
    pk_out,
    pk_in,
    pkm_in,
    ask,
    req,
    ask_row,
    req_row,
    gather_oh,
    own_oh,
    rim_oh,
    xs,
    xr,
    yv,
    yr,
    msg,
    msg_in,
    part,
    parts,
    bytes_of,
    sent,
    halo_recv,
    ask_recv,
    near_recv,
    rim_recv,
    red_recv,
    load_sem,
):
    lon_n, lat_n, fld_n = sizes
    row_n = lat_n * fld_n
    dev_n = lon_n * row_n
    fields, rows, cols = bg.shape
    tile_n, obs_len, patch = tiles.shape
    ext = cols + 2 * EDGE
    per_row = cols // patch
    patch_n = fields * rows * per_row
    pos_n = lon_n * SLOT_ROWS
    bf16, f32, i32 = jnp.bfloat16, jnp.float32, jnp.int32

    my_lon = lax.axis_index("lon")
    my_row = lax.axis_index("lat") * fld_n + lax.axis_index("fld")
    me = my_lon * row_n + my_row

    def device(lon, row):
        return {"lon": lon, "lat": row // fld_n, "fld": row % fld_n}

    west, east = (my_lon + lon_n - 1) % lon_n, (my_lon + 1) % lon_n
    north, south = (my_row + row_n - 1) % row_n, (my_row + 1) % row_n
    has_north = my_row > 0
    has_south = my_row < row_n - 1

    loads = [
        pltpu.make_async_copy(src, dst, load_sem.at[k])
        for k, src, dst in (
            (0, owner_hbm, owner_s),
            (1, slot_hbm, slot_s),
            (2, counts_hbm, counts_s),
            (3, swath_hbm, swath_s),
            (4, scale_hbm, scale_s),
            (5, coupling_hbm, coupling_s),
            (6, values_hbm, obs_values),
            (7, weights_hbm, obs_weights),
            (8, tiles_hbm, tiles),
            (9, edge_hbm, edge),
            (9, bg_hbm, bg),
            (9, decay_hbm, decay),
        )
    ]
    for load in loads:
        load.start()

    barrier = pltpu.get_barrier_semaphore()

    def greet(k):
        other = (me + k) % dev_n
        pl.semaphore_signal(
            barrier, inc=1, device_id=device(other // row_n, other % row_n), device_id_type=MESH
        )

    loop(1, dev_n, greet)

    center = slice(EDGE, EDGE + cols)
    lane8 = lax.broadcasted_iota(i32, (rows, EDGE), 1)
    sub_e = lax.broadcasted_iota(i32, (rows, ext), 0)
    top, bottom = sub_e == 0, sub_e == rows - 1
    rim_mask = ((sub_e < 2) & has_south) | ((sub_e >= rows - 2) & has_north)

    def remote_start(src, dst, recv_sem, lon, row):
        pltpu.make_async_remote_copy(
            src_ref=src,
            dst_ref=dst,
            send_sem=sent.at[0],
            recv_sem=recv_sem,
            device_id=device(lon, row),
            device_id_type=MESH,
        ).start()

    def wait_rows(count, sem):
        some = bytes_of.at[pl.ds(0, count)]
        pltpu.make_async_copy(some, some, sem).wait()

    band_rows = 2 * fields * 2 * cols // 128
    pack_rows = 2 * rows + 4 * 2
    x_rows = (lon_n - 1) * CAP * patch // 128
    y_rows = (lon_n - 1) * pos_n * patch // 256
    msg_rows = 2 * lon_n * 2 * SLOT_ROWS * patch // 256
    ask_rows = (lon_n - 1) * SLOT_ROWS + 3 * lon_n - 1
    sum_rows = (dev_n - 1) * 2

    def turn(value, by):
        return pltpu.roll(value, by % EDGE, 1) if by % EDGE else value

    first_two, last_two = pl.ds(0, 2), pl.ds(rows - 2, 2)

    def halo_start(h):
        pairs = [
            (pk_out.at[h, 0], pk_in.at[h, 1], west, my_row),
            (pk_out.at[h, 1], pk_in.at[h, 0], east, my_row),
            (pk_out.at[h, 0, first_two], pkm_in.at[h, 1, first_two], west, north),
            (pk_out.at[h, 1, first_two], pkm_in.at[h, 0, first_two], east, north),
            (pk_out.at[h, 0, last_two], pkm_in.at[h, 1, last_two], west, south),
            (pk_out.at[h, 1, last_two], pkm_in.at[h, 0, last_two], east, south),
        ]
        if h == 0:
            bands = [(bg, raw_m.at[0]), (edge, raw_m.at[1]), (decay, raw_m.at[2])]
        else:
            bands = [(qs.at[h - 1], qm.at[h - 1])]
        for src, dst in bands:
            pairs.append((src.at[:, first_two], dst.at[:, first_two], my_lon, north))
            pairs.append((src.at[:, last_two], dst.at[:, last_two], my_lon, south))
        sem = halo_recv.at[0] if h == 0 else rim_recv.at[h - 1]
        for src, dst, lon, row in pairs:
            remote_start(src, dst, sem, lon, row)

    def pack(h, values):
        to_west = jnp.zeros((rows, EDGE), f32)
        to_east = to_west
        for g, value in enumerate(values):
            here = lane8 // 2 == g
            to_west = jnp.where(here, turn(value[:, 0:EDGE], 2 * g), to_west)
            to_east = jnp.where(here, turn(value[:, cols - EDGE : cols], 2 * g + 2), to_east)
        pk_out[h, 0] = to_west
        pk_out[h, 1] = to_east

    def west_part(buffer, h, g):
        return turn(buffer[h, 0], EDGE - 2 - 2 * g)

    def east_part(buffer, h, g):
        return turn(buffer[h, 1], EDGE - 2 * g)

    def widened(value, h, g):
        return jnp.concatenate([west_part(pk_in, h, g), value, east_part(pk_in, h, g)], axis=1)

    def widened_m(value, h, g):
        wide = jnp.concatenate([west_part(pkm_in, h, g), value, east_part(pkm_in, h, g)], axis=1)
        return jnp.where(rim_mask, wide, 0.0)

    def y_put(i, value):
        pos_half = lax.broadcasted_iota(i32, (pos_n, patch), 0) % SLOT_ROWS < CAP
        high = value.astype(bf16).astype(f32)
        both = jnp.where(pos_half, high, value - high)
        full = both.astype(bf16)
        yv[i] = full
        yr[i, my_lon] = full
        if i < ITERS:
            blocks = [both[l * SLOT_ROWS : (l + 1) * SLOT_ROWS] for l in range(lon_n)]
            for l in range(lon_n):
                rim = jnp.concatenate(
                    [blocks[l - 1][:, patch - EDGE :], blocks[(l + 1) % lon_n][:, :EDGE]], axis=1
                )
                msg[i, l] = jnp.concatenate([blocks[l], rim], axis=0).astype(bf16)

    def y_start(i):
        def send(k):
            remote_start(
                yv.at[i], yr.at[i, my_lon], near_recv.at[i], (my_lon + k) % lon_n, my_row
            )

        loop(1, lon_n, send)
        if i < ITERS:

            def send_rim(k):
                to = (my_lon + k) % lon_n
                remote_start(msg.at[i, to], msg_in.at[i, 1, my_lon], rim_recv.at[i], to, north)
                remote_start(msg.at[i, to], msg_in.at[i, 0, my_lon], rim_recv.at[i], to, south)

            loop(0, lon_n, send_rim)

    def x_start(i):
        def send(k):
            to = (my_lon + k) % lon_n
            remote_start(
                xs.at[i, to, pl.ds(0, CAP)],
                xr.at[i, my_lon, pl.ds(0, CAP)],
                near_recv.at[i],
                to,
                my_row,
            )

        loop(1, lon_n, send)

    def total_start(k, value):
        part[k] = value
        parts[k, me] = value

        def send(j):
            other = (me + j) % dev_n
            remote_start(
                part.at[k], parts.at[k, me], red_recv.at[k], other // row_n, other % row_n
            )

        loop(1, dev_n, send)

    def total(k):
        wait_rows(sum_rows, red_recv.at[k])
        sums = jnp.sum(parts[k], axis=0)
        return (
            jnp.sum(sums[:, 0:128], axis=1, keepdims=True),
            jnp.sum(sums[:, 128:256], axis=1, keepdims=True),
        )

    def lanes_of(value):
        lane_sum = value[:, 0:128]
        for k in range(1, value.shape[1] // 128):
            lane_sum = lane_sum + value[:, k * 128 : (k + 1) * 128]
        return jnp.sum(lane_sum, axis=0, keepdims=True)

    def mixed(values, f):
        acc = coupling_s[f, 0] * values[0]
        for g in range(1, fields):
            acc = acc + coupling_s[f, g] * values[g]
        return acc

    for load in loads[:8]:
        load.wait()

    pos_row = lax.broadcasted_iota(i32, (pos_n, 128), 0)
    row_lane = lax.broadcasted_iota(i32, (8, 128), 1)
    tile_row = lax.broadcasted_iota(i32, (tile_n, obs_len), 0)
    obs_lane = lax.broadcasted_iota(i32, (tile_n, obs_len), 1)
    holds = jnp.full((pos_n, 128), -1, i32)
    asked = jnp.full((pos_n, 128), -2, i32)
    asked_row = jnp.full((8, 128), -1, i32)
    scale_of = jnp.zeros((tile_n, obs_len), f32)
    count_of = jnp.zeros((tile_n, obs_len), i32)
    for t in range(tile_n):
        rank = jnp.int32(0)
        for other in range(t):
            rank = rank + (owner_s[other] == owner_s[t]).astype(i32)
        number = slot_s[t]
        column, rest = number % per_row, number // per_row
        moved = (column * fields + rest // rows) * rows + rest % rows
        place = owner_s[t] * SLOT_ROWS + rank
        here = (pos_row == place) | (pos_row == place + CAP)
        here_row = (row_lane == place) | (row_lane == place + CAP)
        holds = jnp.where(here, t, holds)
        asked = jnp.where(here, moved, asked)
        asked_row = jnp.where(here_row, moved, asked_row)
        scale_of = jnp.where(tile_row == t, scale_s[swath_s[t]], scale_of)
        count_of = jnp.where(tile_row == t, counts_s[t], count_of)
    tile_of[...] = jnp.concatenate([holds] * (patch // 128), axis=1)
    ask[...] = asked.reshape(lon_n, SLOT_ROWS, 128)
    req[my_lon] = ask[my_lon]
    ask_row[...] = asked_row[0:1]
    req_row[lon_n + my_lon] = asked_row[0:1]
    weight = jnp.where(obs_lane < count_of, obs_weights[...] * scale_of, 0.0)
    weight_high = weight.astype(bf16).astype(f32)
    w_parts[...] = jnp.concatenate([weight_high, weight - weight_high], axis=0).astype(bf16)
    q_rows[...] = (weight * obs_values[...]).astype(bf16).astype(f32)

    def spread(value, t):
        return jnp.where(tile_of[...] == t, value, 0.0).astype(bf16)

    loads[8].wait()
    acc = None
    for t in range(tile_n):
        term = jnp.dot(
            spread(q_rows[t : t + 1, :], t), tiles[t], preferred_element_type=f32
        )
        acc = term if acc is None else acc + term
    y_put(0, acc)

    pick_row = lax.broadcasted_iota(i32, (2 * tile_n, 128), 0) % tile_n

    def gram_of(t, carry):
        chosen = jnp.where(pick_row == t, 1.0, 0.0).astype(bf16)
        column = lax.dot_general(
            w_parts[...], chosen, (((0,), (0,)), ((), ())), preferred_element_type=f32
        )
        tile = tiles[t]
        scaled = (tile.astype(f32) * jnp.concatenate([column] * (patch // 128), axis=1)).astype(bf16)
        gram[t] = lax.dot_general(
            tile, scaled, (((0,), (0,)), ((), ())), preferred_element_type=f32
        ).astype(bf16)
        return carry

    lax.fori_loop(0, GRAMS_AHEAD, gram_of, 0)

    pltpu.make_async_copy(raw_m, raw_m, load_sem.at[9]).wait()
    pack(0, [bg[f] for f in range(fields)] + [edge[e] for e in range(4)] + [decay[f] for f in range(fields)])

    pl.semaphore_wait(barrier, dev_n - 1)
    halo_start(0)

    def send_ask(k):
        to = (my_lon + k) % lon_n
        remote_start(ask.at[to], req.at[my_lon], ask_recv.at[0], to, my_row)
        remote_start(ask_row, req_row.at[lon_n + my_lon], ask_recv.at[0], to, my_row)

    def send_ask_rim(k):
        to = (my_lon + k) % lon_n
        remote_start(ask_row, req_row.at[2 * lon_n + my_lon], ask_recv.at[0], to, north)
        remote_start(ask_row, req_row.at[my_lon], ask_recv.at[0], to, south)

    loop(1, lon_n, send_ask)
    loop(0, lon_n, send_ask_rim)

    y_start(0)
    lax.fori_loop(GRAMS_AHEAD, GRAMS_NEXT, gram_of, 0)

    wait_rows(pack_rows + 3 * band_rows, halo_recv.at[0])
    w = [widened(edge[e], 0, 4 + e) for e in range(4)]
    wm = [widened_m(raw_m[1, e], 0, 4 + e) for e in range(4)]

    def around(main, rim):
        m1, r1 = pltpu.roll(main, 1, 0), pltpu.roll(rim, 1, 0)
        m7, r7 = pltpu.roll(main, rows - 1, 0), pltpu.roll(rim, rows - 1, 0)
        return (
            jnp.where(top, r1, m1),
            jnp.where(bottom, r7, m7),
            jnp.where(top, m1, r1),
            jnp.where(bottom, m7, r7),
        )

    near = [around(w[e], wm[e]) for e in range(4)]

    def coefficients(here, up, down, coef_ref, diag_ref, decays):
        w_west = {e: pltpu.roll(here[e], 1, 1) for e in (0, 2, 3)}
        w_east = {e: pltpu.roll(here[e], ext - 1, 1) for e in (0, 2, 3)}
        e0, e1, e2 = (
            0.5 * (w_west[0] + here[0]),
            0.5 * (w_west[3] + up[3]),
            0.5 * (w_west[2] + down[2]),
        )
        v0, v1, v2 = (
            0.5 * (w_east[0] + here[0]),
            0.5 * (w_east[2] + up[2]),
            0.5 * (w_east[3] + down[3]),
        )
        n0, n1 = 0.5 * (here[1] + up[1]), 0.5 * (here[1] + down[1])
        for k, value in enumerate((e0, e1, e2, v0, v1, v2, n0, n1)):
            coef_ref[k] = value
        degree = (
            n0 + n1 + pltpu.roll(e0 + e1 + e2, ext - 1, 1) + pltpu.roll(v0 + v1 + v2, 1, 1)
        )
        for f in range(fields):
            diag_ref[f] = decays[f] + degree

    coefficients(
        w,
        [near[e][0] for e in range(4)],
        [near[e][1] for e in range(4)],
        coef,
        diag,
        [widened(decay[f], 0, 8 + f) for f in range(fields)],
    )
    coefficients(
        wm,
        [near[e][2] for e in range(4)],
        [near[e][3] for e in range(4)],
        coef_m,
        diag_m,
        [widened_m(raw_m[2, f], 0, 8 + f) for f in range(fields)],
    )

    def apply_l(c, d, value, up, down):
        toward_east = c[0] * value + c[1] * up + c[2] * down
        toward_west = c[3] * value + c[4] * up + c[5] * down
        result = d * value - c[6] * up - c[7] * down
        return result - pltpu.roll(toward_east, ext - 1, 1) - pltpu.roll(toward_west, 1, 1)

    def first_pass(main, rim):
        out, out_m = [], []
        for f in range(fields):
            up, down, up_m, down_m = around(main[f], rim[f])
            out.append(apply_l(coef, diag[f], main[f], up, down))
            out_m.append(apply_l(coef_m, diag_m[f], rim[f], up_m, down_m))
        return out, out_m

    def second_pass(h, first, first_m):
        u = [mixed(first, f) for f in range(fields)]
        um = [jnp.where(rim_mask, mixed(first_m, f), 0.0) for f in range(fields)]
        for f in range(fields):
            up, down, _, _ = around(u[f], um[f])
            qs[h, f] = apply_l(coef, diag[f], u[f], up, down)[:, center]
        return u

    def send_q(h):
        pack(h + 1, [qs[h, f] for f in range(fields)])
        stacked = jnp.concatenate(
            [
                qs[h, f, :, c * patch : (c + 1) * patch]
                for c in range(per_row)
                for f in range(fields)
            ],
            axis=0,
        )
        high = stacked.astype(bf16)
        low = (stacked - high.astype(f32)).astype(bf16)
        chosen = gather_oh[...]
        patches = jnp.dot(chosen, low, preferred_element_type=f32) + jnp.dot(
            chosen, high, preferred_element_type=f32
        )
        xs[h] = patches.reshape(lon_n, SLOT_ROWS, patch)
        x_start(h)
        halo_start(h + 1)
        xr[h, my_lon] = xs[h, my_lon]

    main = [widened(bg[f], 0, f) for f in range(fields)]
    rim = [widened_m(raw_m[0, f], 0, f) for f in range(fields)]
    first, first_m = first_pass(main, rim)
    second_pass(0, first, first_m)

    wait_rows(ask_rows, ask_recv.at[0])
    wanted = req[...].reshape(pos_n, 128)
    wanted = jnp.concatenate([wanted] * (patch_n // 128), axis=1)
    picked = wanted == lax.broadcasted_iota(i32, (pos_n, patch_n), 1)
    gather_oh[...] = jnp.where(picked, 1.0, 0.0).astype(bf16)
    send_q(0)

    lane1 = lax.broadcasted_iota(i32, (1, 128), 1)
    own_k, rim_k = lon_n * pos_n, 2 * lon_n * 2 * SLOT_ROWS

    def iota(n, axis):
        return lax.broadcasted_iota(i32, (n, 128), axis)

    own_rows = iota(patch_n, 0)
    side_rows = iota(fields * rows, 0)
    for group in range(own_k // 128):
        slots = jnp.full((1, 128), -1, i32)
        for h in range(lon_n):
            if h * pos_n // 128 == group:
                offset = h * pos_n % 128
                moved = turn(req_row[lon_n + h], offset)
                slots = jnp.where((lane1 >= offset) & (lane1 < offset + pos_n), moved, slots)
        lanes = slice(group * 128, (group + 1) * 128)
        at = lane1 % pos_n // SLOT_ROWS

        def match(rows_of, owner):
            wanted = jnp.where(at == owner, slots, -1)
            return jnp.where(rows_of == wanted, 1.0, 0.0).astype(bf16)

        own_oh[0:patch_n, lanes] = match(own_rows, my_lon)
        first_side, last_side = patch_n, patch_n + fields * rows
        own_oh[first_side:last_side, lanes] = match(
            (per_row - 1) * fields * rows + side_rows, west
        )
        own_oh[last_side : last_side + fields * rows, lanes] = match(side_rows, east)
        tile_rows = last_side + fields * rows
        mine = (iota(pos_n, 0) // SLOT_ROWS == at) & (ask[...].reshape(pos_n, 128) == slots)
        own_oh[tile_rows : tile_rows + pos_n, lanes] = jnp.where(mine, 1.0, 0.0).astype(bf16)

    for group in range(rim_k // 128):
        ours = jnp.full((1, 128), -1, i32)
        from_west, from_east = ours, ours
        side = group * 128 // (rim_k // 2)
        for index in range(2 * lon_n):
            if index * 2 * SLOT_ROWS // 128 != group:
                continue
            offset = index * 2 * SLOT_ROWS % 128
            table = jnp.broadcast_to(
                req_row[(index // lon_n) * 2 * lon_n + index % lon_n], (8, 128)
            )
            low = (lane1 >= offset) & (lane1 < offset + SLOT_ROWS)
            high = (lane1 >= offset + SLOT_ROWS) & (lane1 < offset + 2 * SLOT_ROWS)

            def brought(owner, to):
                by = (to - owner * SLOT_ROWS + 2 * 128) % 128
                return pltpu.roll(table, by, 1)[0:1]

            ours = jnp.where(low, brought(my_lon, offset), ours)
            from_west = jnp.where(high, brought(west, offset + SLOT_ROWS), from_west)
            from_east = jnp.where(high, brought(east, offset + SLOT_ROWS), from_east)
        lanes = slice(group * 128, (group + 1) * 128)
        is_north = (group * 128 + lane1) < rim_k // 2

        def match_rim(row_ids, wanted):
            sub = row_ids % rows
            keep = (is_north & has_north & (sub >= rows - 2)) | (
                (~is_north) & has_south & (sub < 2)
            )
            return jnp.where(keep & (row_ids == wanted), 1.0, 0.0).astype(bf16)

        rim_oh[0:patch_n, lanes] = match_rim(own_rows, ours)
        rim_oh[patch_n : patch_n + fields * rows, lanes] = match_rim(
            (per_row - 1) * fields * rows + side_rows, from_west
        )
        rim_oh[patch_n + fields * rows :, lanes] = match_rim(side_rows, from_east)

    lax.fori_loop(GRAMS_NEXT, tile_n, gram_of, 0)

    pos_sub = lax.broadcasted_iota(i32, (pos_n, patch), 0) % SLOT_ROWS

    def placed_field(blocks, f):
        return jnp.concatenate(
            [
                blocks[(c * fields + f) * rows : (c * fields + f + 1) * rows]
                for c in range(per_row)
            ],
            axis=1,
        )

    def received(h):
        wait_rows(x_rows + y_rows, near_recv.at[h])
        blocks = jnp.dot(
            own_oh[...], yr[h].reshape(own_k, patch), preferred_element_type=f32
        )
        came = xr[h].reshape(pos_n, patch)
        came = jnp.where(pos_sub < CAP, came, pltpu.roll(came, CAP, 0))
        seen = came + blocks[patch_n + 2 * fields * rows :]
        return seen, blocks

    def assembled(h, blocks):
        wait_rows(pack_rows + band_rows + msg_rows, rim_recv.at[h])
        rim_blocks = jnp.dot(
            rim_oh[...], msg_in[h].reshape(rim_k, patch), preferred_element_type=f32
        )
        main, rim = [], []
        for f in range(fields):
            west_rows = slice(patch_n + f * rows, patch_n + (f + 1) * rows)
            east_rows = slice(patch_n + (fields + f) * rows, patch_n + (fields + f + 1) * rows)
            main.append(
                jnp.concatenate(
                    [
                        west_part(pk_in, h + 1, f) + blocks[west_rows, patch - EDGE :],
                        qs[h, f] + placed_field(blocks, f),
                        east_part(pk_in, h + 1, f) + blocks[east_rows, :EDGE],
                    ],
                    axis=1,
                )
            )
            rim.append(
                widened_m(qm[h, f], h + 1, f)
                + jnp.concatenate(
                    [
                        rim_blocks[west_rows, :EDGE],
                        placed_field(rim_blocks, f),
                        rim_blocks[east_rows, patch - EDGE :],
                    ],
                    axis=1,
                )
            )
        return main, rim

    def tile_images(seen):
        high = seen.astype(bf16).astype(f32)
        both = jnp.where(pos_sub < CAP, high, seen - high)
        acc = None
        for t in range(tile_n):
            term = jnp.dot(spread(both, t), gram[t], preferred_element_type=f32)
            acc = term if acc is None else acc + term
        swapped = pltpu.roll(acc.reshape(lon_n, SLOT_ROWS, patch), CAP, 1)
        return acc + swapped.reshape(pos_n, patch)

    seen, blocks = received(0)
    moments = []
    tau = None
    for it in range(ITERS):
        last = it == ITERS - 1
        images = tile_images(seen)
        y_put(it + 1, images)
        y_start(it + 1)
        main, rim = assembled(it, blocks)
        if it == 2:
            main, rim = [tau * v for v in main], [tau * v for v in rim]
        for f in range(fields):
            vecs[it, f], vec_m[f] = main[f], rim[f]
        main = [vecs[it, f] for f in range(fields)]
        rim = [vec_m[f] for f in range(fields)]
        first, first_m = first_pass(main, rim)
        u = [mixed(first, f)[:, center] for f in range(fields)]
        even = jnp.zeros((1, 128), f32)
        odd = lanes_of(jnp.where(pos_sub < CAP, seen * images, 0.0))
        for f in range(fields):
            here = main[f][:, center]
            even = even + lanes_of(here * here)
            odd = odd + lanes_of(u[f] * first[f][:, center])
        total_start(it, jnp.concatenate([even, odd], axis=1))
        second_pass(it + 1, first, first_m)
        if not last:
            send_q(it + 1)
            seen, blocks = received(it + 1)
            if it == 1:
                moments.append(total(0))
                tau = moments[0][0] / moments[0][1]
                seen = tau * seen
    wait_rows(y_rows, near_recv.at[ITERS])
    blocks = jnp.dot(
        own_oh[0:patch_n, :], yr[ITERS].reshape(own_k, patch), preferred_element_type=f32
    )

    m2, m3 = total(1)
    scale = 1.0 / moments[0][0]
    g2, g3 = tau * tau * m2 * scale, tau * tau * tau * m3 * scale
    beta0 = g2 - 1.0
    c0 = 1.0 + beta0
    alpha1 = beta0 / (c0 * c0 - 2.0 * c0 * g2 + g3)
    a1, a2 = -1.0 - alpha1 * c0, alpha1
    m4, m5 = total(2)
    g4, g5 = tau * tau * m4 * scale, tau * tau * tau * m5 * scale
    gamma2 = 1.0 + 2.0 * a1 + (a1 * a1 + 2.0 * a2) * g2 + 2.0 * a1 * a2 * g3 + a2 * a2 * g4
    beta1 = gamma2 / beta0
    b0, b1, b2 = 1.0 + beta1 * c0, a1 - beta1, a2
    alpha2 = gamma2 / (
        b0 * b0
        + 2.0 * b0 * b1 * g2
        + (b1 * b1 + 2.0 * b0 * b2) * g3
        + 2.0 * b1 * b2 * g4
        + b2 * b2 * g5
    )
    x0, x1, x2 = (
        tau * (1.0 + alpha1 * c0 + alpha2 * b0),
        tau * tau * (alpha2 * b1 - alpha1),
        tau * tau * (alpha2 * b2),
    )
    r1, r2, r3 = tau * (a1 - alpha2 * b0), tau * (a2 - alpha2 * b1), -tau * tau * (alpha2 * b2)
    for f in range(fields):
        e0, e1, e2 = (vecs[it, f, :, center] for it in range(ITERS))
        sol_out[f] = x0 * e0 + x1 * e1 + x2 * e2
        res_out[f] = e0 + r1 * e1 + r2 * e2 + r3 * (qs[ITERS, f] + placed_field(blocks, f))

    wait_rows(sent_rows(sizes, bg.shape, patch), sent.at[0])


def sent_rows(sizes, shape, patch):
    lon_n, lat_n, fld_n = sizes
    fields, rows, cols = shape
    dev_n, pos_n = lon_n * lat_n * fld_n, lon_n * SLOT_ROWS
    halos = (ITERS + 1) * (2 * rows + 8) + (3 + ITERS) * 4 * fields * cols // 128
    asks = (lon_n - 1) * SLOT_ROWS + 3 * lon_n - 1
    inputs = ITERS * (lon_n - 1) * CAP * patch // 128
    images = (ITERS + 1) * (lon_n - 1) * pos_n * patch // 256
    rims = ITERS * 2 * lon_n * 2 * SLOT_ROWS * patch // 256
    return halos + asks + inputs + images + rims + ITERS * (dev_n - 1) * 2


def on_device(
    sizes,
    background,
    decay_sq,
    edge_weight,
    coupling,
    obs_tiles,
    obs_values,
    obs_weights,
    obs_counts,
    swath_ids,
    swath_scale,
    tile_owner,
    tile_slot,
):
    fields, rows, cols = background.shape
    tile_n, obs_len, patch = obs_tiles.shape
    lon_n, lat_n, fld_n = sizes
    dev_n = lon_n * lat_n * fld_n
    ext = cols + 2 * EDGE
    pos_n = lon_n * SLOT_ROWS
    patch_n = fields * rows * cols // patch
    side_n = 2 * fields * rows
    halos = ITERS + 1
    f32, bf16, i32 = jnp.float32, jnp.bfloat16, jnp.int32
    vmem = pl.BlockSpec(memory_space=pltpu.VMEM)
    dma = pltpu.SemaphoreType.DMA
    shape = pltpu.VMEM((fields, rows, cols), f32)
    block = pltpu.VMEM((fields, rows, ext), f32)
    return pl.pallas_call(
        functools.partial(kernel, sizes),
        out_shape=(shape, shape),
        in_specs=[pl.BlockSpec(memory_space=pltpu.HBM)] * 12,
        out_specs=(vmem, vmem),
        scratch_shapes=[
            pltpu.SMEM(tile_owner.shape, i32),
            pltpu.SMEM(tile_slot.shape, i32),
            pltpu.SMEM(obs_counts.shape, i32),
            pltpu.SMEM(swath_ids.shape, i32),
            pltpu.SMEM(swath_scale.shape, f32),
            pltpu.SMEM(coupling.shape, f32),
            pltpu.VMEM(background.shape, f32),
            pltpu.VMEM(decay_sq.shape, f32),
            pltpu.VMEM(edge_weight.shape, f32),
            pltpu.VMEM(obs_values.shape, f32),
            pltpu.VMEM(obs_weights.shape, f32),
            pltpu.VMEM((tile_n, obs_len, patch), bf16),
            pltpu.VMEM((tile_n, patch, patch), bf16),
            pltpu.VMEM((2 * tile_n, obs_len), bf16),
            pltpu.VMEM((tile_n, obs_len), f32),
            pltpu.VMEM((pos_n, patch), i32),
            pltpu.VMEM((8, rows, ext), f32),
            pltpu.VMEM((8, rows, ext), f32),
            block,
            block,
            pltpu.VMEM((ITERS, fields, rows, ext), f32),
            block,
            pltpu.VMEM((ITERS + 1, fields, rows, cols), f32),
            pltpu.VMEM((ITERS, fields, rows, cols), f32),
            pltpu.VMEM((3, fields, rows, cols), f32),
            pltpu.VMEM((halos, 2, rows, EDGE), f32),
            pltpu.VMEM((halos, 2, rows, EDGE), f32),
            pltpu.VMEM((halos, 2, rows, EDGE), f32),
            pltpu.VMEM((lon_n, SLOT_ROWS, 128), i32),
            pltpu.VMEM((lon_n, SLOT_ROWS, 128), i32),
            pltpu.VMEM((1, 128), i32),
            pltpu.VMEM((3 * lon_n, 1, 128), i32),
            pltpu.VMEM((pos_n, patch_n), bf16),
            pltpu.VMEM((patch_n + side_n + pos_n, lon_n * pos_n), bf16),
            pltpu.VMEM((patch_n + side_n, 4 * lon_n * SLOT_ROWS), bf16),
            pltpu.VMEM((ITERS, lon_n, SLOT_ROWS, patch), f32),
            pltpu.VMEM((ITERS, lon_n, SLOT_ROWS, patch), f32),
            pltpu.VMEM((ITERS + 1, pos_n, patch), bf16),
            pltpu.VMEM((ITERS + 1, lon_n, pos_n, patch), bf16),
            pltpu.VMEM((ITERS, lon_n, 2 * SLOT_ROWS, patch), bf16),
            pltpu.VMEM((ITERS, 2, lon_n, 2 * SLOT_ROWS, patch), bf16),
            pltpu.VMEM((ITERS, 1, 256), f32),
            pltpu.VMEM((ITERS, dev_n, 1, 256), f32),
            pltpu.VMEM((sent_rows(sizes, background.shape, patch), 128), f32),
            dma((1,)),
            dma((1,)),
            dma((1,)),
            dma((ITERS + 1,)),
            dma((ITERS,)),
            dma((ITERS,)),
            dma((10,)),
        ],
        compiler_params=pltpu.CompilerParams(
            collective_id=0, has_side_effects=True, vmem_limit_bytes=67043328 - 3 * 2**20
        ),
    )(
        tile_owner,
        tile_slot,
        obs_counts,
        swath_ids,
        swath_scale,
        coupling,
        background,
        decay_sq,
        edge_weight,
        obs_tiles,
        obs_values,
        obs_weights,
    )


def solution(mesh):
    sizes = (mesh.shape["lon"], mesh.shape["lat"], mesh.shape["fld"])
    return jax.shard_map(
        functools.partial(on_device, sizes),
        mesh=mesh,
        in_specs=(
            P("group", ("lat", "fld"), "lon"),
            P(None, ("lat", "fld"), "lon"),
            P(None, ("lat", "fld"), "lon"),
            P(),
            P(("lon", "lat", "fld"), None, None),
            P(("group", "lon", "lat", "fld"), None),
            P(("lon", "lat", "fld"), None),
            P(("lon", "lat", "fld")),
            P(("lon", "lat", "fld")),
            P(),
            P(("lon", "lat", "fld")),
            P(("lon", "lat", "fld")),
        ),
        out_specs=(P("group", ("lat", "fld"), "lon"), P("group", ("lat", "fld"), "lon")),
        check_vma=False,
    )
```

```python
import functools

import jax
import jax.numpy as jnp
from jax import lax
from jax.experimental import pallas as pl
from jax.experimental.pallas import tpu as pltpu
from jax.sharding import PartitionSpec as P

CAP = 4
ITERS = 3
SLOT_ROWS = 8
EDGE = 128
GRAMS_AHEAD = 5
GRAMS_NEXT = 13
MESH = pl.DeviceIdType.MESH


def loop(low, high, body):
    if high - low <= 16:
        for k in range(low, high):
            body(k)
    else:
        lax.fori_loop(low, high, lambda k, c: (body(k), c)[1], 0)


def kernel(
    sizes,
    owner_hbm,
    slot_hbm,
    counts_hbm,
    swath_hbm,
    scale_hbm,
    coupling_hbm,
    bg_hbm,
    decay_hbm,
    edge_hbm,
    tiles_hbm,
    values_hbm,
    weights_hbm,
    sol_out,
    res_out,
    owner_s,
    slot_s,
    counts_s,
    swath_s,
    scale_s,
    coupling_s,
    bg,
    decay,
    edge,
    obs_values,
    obs_weights,
    tiles,
    gram,
    w_parts,
    q_rows,
    tile_of,
    coef,
    coef_m,
    diag,
    diag_m,
    vecs,
    vec_m,
    qs,
    qm,
    raw_m,
    pk_out,
    pk_in,
    pkm_in,
    ask,
    req,
    ask_row,
    req_row,
    gather_oh,
    own_oh,
    rim_oh,
    xs,
    xr,
    yv,
    yr,
    msg,
    msg_in,
    part,
    parts,
    bytes_of,
    sent,
    halo_recv,
    ask_recv,
    near_recv,
    rim_recv,
    red_recv,
    load_sem,
):
    lon_n, lat_n, fld_n = sizes
    row_n = lat_n * fld_n
    dev_n = lon_n * row_n
    fields, rows, cols = bg.shape
    tile_n, obs_len, patch = tiles.shape
    ext = cols + 2 * EDGE
    per_row = cols // patch
    patch_n = fields * rows * per_row
    pos_n = lon_n * SLOT_ROWS
    bf16, f32, i32 = jnp.bfloat16, jnp.float32, jnp.int32

    my_lon = lax.axis_index("lon")
    my_row = lax.axis_index("lat") * fld_n + lax.axis_index("fld")
    me = my_lon * row_n + my_row

    def device(lon, row):
        return {"lon": lon, "lat": row // fld_n, "fld": row % fld_n}

    west, east = (my_lon + lon_n - 1) % lon_n, (my_lon + 1) % lon_n
    north, south = (my_row + row_n - 1) % row_n, (my_row + 1) % row_n
    has_north = my_row > 0
    has_south = my_row < row_n - 1
    inner = has_north & has_south

    loads = [
        pltpu.make_async_copy(src, dst, load_sem.at[k])
        for k, src, dst in (
            (0, owner_hbm, owner_s),
            (1, slot_hbm, slot_s),
            (2, counts_hbm, counts_s),
            (3, swath_hbm, swath_s),
            (4, scale_hbm, scale_s),
            (5, coupling_hbm, coupling_s),
            (6, values_hbm, obs_values),
            (7, weights_hbm, obs_weights),
            (8, tiles_hbm, tiles),
            (9, edge_hbm, edge),
            (9, bg_hbm, bg),
            (9, decay_hbm, decay),
        )
    ]
    for load in loads:
        load.start()

    barrier = pltpu.get_barrier_semaphore()

    def greet(k):
        other = (me + k) % dev_n
        pl.semaphore_signal(
            barrier, inc=1, device_id=device(other // row_n, other % row_n), device_id_type=MESH
        )

    for side, there in ((0, has_north), (1, has_south)):

        @pl.when(jnp.logical_not(there))
        def _():
            for i in range(ITERS):
                msg_in[i, side] = jnp.zeros(msg_in.shape[2:], bf16)

    loop(1, dev_n, greet)

    center = slice(EDGE, EDGE + cols)
    lane8 = lax.broadcasted_iota(i32, (rows, EDGE), 1)
    sub_e = lax.broadcasted_iota(i32, (rows, ext), 0)
    top, bottom = sub_e == 0, sub_e == rows - 1
    low_half = sub_e < fields
    rim_mask = (low_half & has_north) | ((sub_e >= fields) & has_south)
    edge_mask = ((sub_e < 2) & has_south) | ((sub_e >= rows - 2) & has_north)

    toward = jnp.where(my_lon < lon_n // 2, lon_n - 1, 1)

    def remote_start(src, dst, recv_sem, lon, row):
        pltpu.make_async_remote_copy(
            src_ref=src,
            dst_ref=dst,
            send_sem=sent.at[0],
            recv_sem=recv_sem,
            device_id=device(lon, row),
            device_id_type=MESH,
        ).start()

    def wait_rows(count, sem):
        some = bytes_of.at[pl.ds(0, count)]
        pltpu.make_async_copy(some, some, sem).wait()

    band_rows = 2 * fields * 2 * cols // 128
    pack_rows = 2 * rows + 4 * 2
    x_rows = (lon_n - 1) * CAP * patch // 128
    y_rows = (lon_n - 1) * pos_n * patch // 256
    msg_rows = 2 * lon_n * 2 * SLOT_ROWS * patch // 256
    ask_rows = (lon_n - 1) * SLOT_ROWS + 3 * lon_n - 1
    sum_rows = (dev_n - 1) * 2

    def turn(value, by):
        return pltpu.roll(value, by % EDGE, 1) if by % EDGE else value

    first_two, last_two = pl.ds(0, 2), pl.ds(rows - 2, 2)

    def halo_start(h):
        pairs = [
            (pk_out.at[h, 0], pk_in.at[h, 1], west, my_row),
            (pk_out.at[h, 1], pk_in.at[h, 0], east, my_row),
            (pk_out.at[h, 0, first_two], pkm_in.at[h, 1, first_two], west, north),
            (pk_out.at[h, 1, first_two], pkm_in.at[h, 0, first_two], east, north),
            (pk_out.at[h, 0, last_two], pkm_in.at[h, 1, last_two], west, south),
            (pk_out.at[h, 1, last_two], pkm_in.at[h, 0, last_two], east, south),
        ]
        if h == 0:
            bands = [(bg, raw_m.at[0]), (edge, raw_m.at[1]), (decay, raw_m.at[2])]
        else:
            bands = [(qs.at[h - 1], qm.at[h - 1])]
        for src, dst in bands:
            pairs.append((src.at[:, first_two], dst.at[:, first_two], my_lon, north))
            pairs.append((src.at[:, last_two], dst.at[:, last_two], my_lon, south))
        sem = halo_recv.at[0] if h == 0 else rim_recv.at[h - 1]
        for src, dst, lon, row in pairs:
            remote_start(src, dst, sem, lon, row)

    def pack(h, values):
        to_west = jnp.zeros((rows, EDGE), f32)
        to_east = to_west
        for g, value in enumerate(values):
            here = lane8 // 2 == g
            to_west = jnp.where(here, turn(value[:, 0:EDGE], 2 * g), to_west)
            to_east = jnp.where(here, turn(value[:, cols - EDGE : cols], 2 * g + 2), to_east)
        pk_out[h, 0] = to_west
        pk_out[h, 1] = to_east

    def west_part(buffer, h, g):
        return turn(buffer[h, 0], EDGE - 2 - 2 * g)

    def east_part(buffer, h, g):
        return turn(buffer[h, 1], EDGE - 2 * g)

    def widened(value, h, g):
        return jnp.concatenate([west_part(pk_in, h, g), value, east_part(pk_in, h, g)], axis=1)

    def widened_m(value, h, g):
        return jnp.concatenate([west_part(pkm_in, h, g), value, east_part(pkm_in, h, g)], axis=1)

    def packed(values, north_row, south_row):
        out = pltpu.roll(values[0], -north_row % rows, 0)
        for f in range(1, fields):
            out = jnp.where(sub_e == f, pltpu.roll(values[f], (f - north_row) % rows, 0), out)
        for f in range(fields):
            moved = pltpu.roll(values[f], (fields + f - south_row) % rows, 0)
            out = jnp.where(sub_e == fields + f, moved, out)
        return out

    def rims(values):
        near_rim = packed(values, rows - 1, 0)
        far_rim = packed(values, rows - 2, 1)
        return jnp.where(rim_mask, near_rim, 0.0), jnp.where(rim_mask, far_rim, 0.0)

    def y_put(i, value):
        pos_half = lax.broadcasted_iota(i32, (pos_n, patch), 0) % SLOT_ROWS < CAP
        high = value.astype(bf16).astype(f32)
        both = jnp.where(pos_half, high, value - high)
        full = both.astype(bf16)
        yv[i] = full
        yr[i, my_lon] = full
        if i < ITERS:
            blocks = [both[l * SLOT_ROWS : (l + 1) * SLOT_ROWS] for l in range(lon_n)]
            for l in range(lon_n):
                rim = jnp.concatenate(
                    [blocks[l - 1][:, patch - EDGE :], blocks[(l + 1) % lon_n][:, :EDGE]], axis=1
                )
                msg[i, l] = jnp.concatenate([blocks[l], rim], axis=0).astype(bf16)

    def y_start(i):
        def send(k):
            remote_start(
                yv.at[i], yr.at[i, my_lon], near_recv.at[i], (my_lon + k * toward) % lon_n, my_row
            )

        loop(1, lon_n, send)
        if i < ITERS:

            def send_rim(k):
                to = (my_lon + k * toward) % lon_n

                @pl.when(has_north)
                def _():
                    remote_start(msg.at[i, to], msg_in.at[i, 1, my_lon], rim_recv.at[i], to, north)

                @pl.when(has_south)
                def _():
                    remote_start(msg.at[i, to], msg_in.at[i, 0, my_lon], rim_recv.at[i], to, south)

            loop(0, lon_n, send_rim)

    def x_start(i):
        def send(k):
            to = (my_lon + k * toward) % lon_n
            remote_start(
                xs.at[i, to, pl.ds(0, CAP)],
                xr.at[i, my_lon, pl.ds(0, CAP)],
                near_recv.at[i],
                to,
                my_row,
            )

        loop(1, lon_n, send)

    def total_start(k, value):
        part[k] = value
        parts[k, me] = value

        def send(j):
            other = (me + j) % dev_n
            remote_start(
                part.at[k], parts.at[k, me], red_recv.at[k], other // row_n, other % row_n
            )

        loop(1, dev_n, send)

    def total(k):
        wait_rows(sum_rows, red_recv.at[k])
        sums = jnp.sum(parts[k], axis=0)
        return (
            jnp.sum(sums[:, 0:128], axis=1, keepdims=True),
            jnp.sum(sums[:, 128:256], axis=1, keepdims=True),
        )

    def lanes_of(value):
        lane_sum = value[:, 0:128]
        for k in range(1, value.shape[1] // 128):
            lane_sum = lane_sum + value[:, k * 128 : (k + 1) * 128]
        return jnp.sum(lane_sum, axis=0, keepdims=True)

    def mixed(values, f):
        acc = coupling_s[f, 0] * values[0]
        for g in range(1, fields):
            acc = acc + coupling_s[f, g] * values[g]
        return acc

    for load in loads[:8]:
        load.wait()

    pos_row = lax.broadcasted_iota(i32, (pos_n, 128), 0)
    row_lane = lax.broadcasted_iota(i32, (8, 128), 1)
    tile_row = lax.broadcasted_iota(i32, (tile_n, obs_len), 0)
    obs_lane = lax.broadcasted_iota(i32, (tile_n, obs_len), 1)
    holds = jnp.full((pos_n, 128), -1, i32)
    asked = jnp.full((pos_n, 128), -2, i32)
    asked_row = jnp.full((8, 128), -1, i32)
    scale_of = jnp.zeros((tile_n, obs_len), f32)
    count_of = jnp.zeros((tile_n, obs_len), i32)
    for t in range(tile_n):
        rank = jnp.int32(0)
        for other in range(t):
            rank = rank + (owner_s[other] == owner_s[t]).astype(i32)
        number = slot_s[t]
        column, rest = number % per_row, number // per_row
        moved = (column * fields + rest // rows) * rows + rest % rows
        place = owner_s[t] * SLOT_ROWS + rank
        here = (pos_row == place) | (pos_row == place + CAP)
        here_row = (row_lane == place) | (row_lane == place + CAP)
        holds = jnp.where(here, t, holds)
        asked = jnp.where(here, moved, asked)
        asked_row = jnp.where(here_row, moved, asked_row)
        scale_of = jnp.where(tile_row == t, scale_s[swath_s[t]], scale_of)
        count_of = jnp.where(tile_row == t, counts_s[t], count_of)
    tile_of[...] = jnp.concatenate([holds] * (patch // 128), axis=1)
    ask[...] = asked.reshape(lon_n, SLOT_ROWS, 128)
    req[my_lon] = ask[my_lon]
    ask_row[...] = asked_row[0:1]
    req_row[lon_n + my_lon] = asked_row[0:1]
    weight = jnp.where(obs_lane < count_of, obs_weights[...] * scale_of, 0.0)
    weight_high = weight.astype(bf16).astype(f32)
    w_parts[...] = jnp.concatenate([weight_high, weight - weight_high], axis=0).astype(bf16)
    q_rows[...] = (weight * obs_values[...]).astype(bf16).astype(f32)

    def spread(value, t):
        return jnp.where(tile_of[...] == t, value, 0.0).astype(bf16)

    loads[8].wait()
    acc = None
    for t in range(tile_n):
        term = jnp.dot(
            spread(q_rows[t : t + 1, :], t), tiles[t], preferred_element_type=f32
        )
        acc = term if acc is None else acc + term
    y_put(0, acc)

    pick_row = lax.broadcasted_iota(i32, (2 * tile_n, 128), 0) % tile_n

    def gram_of(t, carry):
        chosen = jnp.where(pick_row == t, 1.0, 0.0).astype(bf16)
        column = lax.dot_general(
            w_parts[...], chosen, (((0,), (0,)), ((), ())), preferred_element_type=f32
        )
        tile = tiles[t]
        scaled = (tile.astype(f32) * jnp.concatenate([column] * (patch // 128), axis=1)).astype(bf16)
        gram[t] = lax.dot_general(
            tile, scaled, (((0,), (0,)), ((), ())), preferred_element_type=f32
        ).astype(bf16)
        return carry

    lax.fori_loop(0, GRAMS_AHEAD, gram_of, 0)

    pltpu.make_async_copy(raw_m, raw_m, load_sem.at[9]).wait()
    pack(0, [bg[f] for f in range(fields)] + [edge[e] for e in range(4)] + [decay[f] for f in range(fields)])

    pl.semaphore_wait(barrier, dev_n - 1)
    halo_start(0)

    def send_ask(k):
        to = (my_lon + k * toward) % lon_n
        remote_start(ask.at[to], req.at[my_lon], ask_recv.at[0], to, my_row)
        remote_start(ask_row, req_row.at[lon_n + my_lon], ask_recv.at[0], to, my_row)

    def send_ask_rim(k):
        to = (my_lon + k * toward) % lon_n
        remote_start(ask_row, req_row.at[2 * lon_n + my_lon], ask_recv.at[0], to, north)
        remote_start(ask_row, req_row.at[my_lon], ask_recv.at[0], to, south)

    loop(1, lon_n, send_ask)
    loop(0, lon_n, send_ask_rim)

    y_start(0)
    lax.fori_loop(GRAMS_AHEAD, GRAMS_NEXT, gram_of, 0)

    wait_rows(pack_rows + 3 * band_rows, halo_recv.at[0])
    w = [widened(edge[e], 0, 4 + e) for e in range(4)]
    wm = [jnp.where(edge_mask, widened_m(raw_m[1, e], 0, 4 + e), 0.0) for e in range(4)]

    def around(main, rim):
        m1, r1 = pltpu.roll(main, 1, 0), pltpu.roll(rim, 1, 0)
        m7, r7 = pltpu.roll(main, rows - 1, 0), pltpu.roll(rim, rows - 1, 0)
        return (
            jnp.where(top, r1, m1),
            jnp.where(bottom, r7, m7),
            jnp.where(top, m1, r1),
            jnp.where(bottom, m7, r7),
        )

    near = [around(w[e], wm[e]) for e in range(4)]

    def coefficients(here, up, down):
        w_west = {e: pltpu.roll(here[e], 1, 1) for e in (0, 2, 3)}
        w_east = {e: pltpu.roll(here[e], ext - 1, 1) for e in (0, 2, 3)}
        e0, e1, e2 = (
            0.5 * (w_west[0] + here[0]),
            0.5 * (w_west[3] + up[3]),
            0.5 * (w_west[2] + down[2]),
        )
        v0, v1, v2 = (
            0.5 * (w_east[0] + here[0]),
            0.5 * (w_east[2] + up[2]),
            0.5 * (w_east[3] + down[3]),
        )
        n0, n1 = 0.5 * (here[1] + up[1]), 0.5 * (here[1] + down[1])
        degree = (
            n0 + n1 + pltpu.roll(e0 + e1 + e2, ext - 1, 1) + pltpu.roll(v0 + v1 + v2, 1, 1)
        )
        return (e0, e1, e2, v0, v1, v2, n0, n1), degree

    values, degree = coefficients(
        w, [near[e][0] for e in range(4)], [near[e][1] for e in range(4)]
    )
    for k, value in enumerate(values):
        coef[k] = value
    for f in range(fields):
        diag[f] = widened(decay[f], 0, 8 + f) + degree
    values, degree = coefficients(
        wm, [near[e][2] for e in range(4)], [near[e][3] for e in range(4)]
    )
    for k, value in enumerate(values):
        coef_m[k] = jnp.where(low_half, value[rows - 1 : rows], value[0:1])
    diag_m[...] = packed(
        [widened_m(raw_m[2, f], 0, 8 + f) + degree for f in range(fields)], rows - 1, 0
    )

    def apply_l(c, d, value, up, down):
        toward_east = c[0] * value + c[1] * up + c[2] * down
        toward_west = c[3] * value + c[4] * up + c[5] * down
        result = d * value - c[6] * up - c[7] * down
        return result - pltpu.roll(toward_east, ext - 1, 1) - pltpu.roll(toward_west, 1, 1)

    lane_row = lax.broadcasted_iota(i32, (rows, 128), 0)
    blends = []
    for d in range(fields):
        blend = jnp.zeros((rows, 128), f32)
        for k in range(rows):
            blend = jnp.where(lane_row == k, coupling_s[k % fields, (k + d) % fields], blend)
        blends.append(jnp.concatenate([blend] * (ext // 128), axis=1))

    def mixed_rim(value):
        acc = blends[0] * value
        for d in range(1, fields):
            ahead = pltpu.roll(value, rows - d, 0)
            behind = pltpu.roll(value, fields - d, 0)
            acc = acc + blends[d] * jnp.where(sub_e % fields < fields - d, ahead, behind)
        return acc

    def beside(value, rim, f):
        up = jnp.where(top, pltpu.roll(rim, -f % rows, 0), pltpu.roll(value, 1, 0))
        down = jnp.where(
            bottom, pltpu.roll(rim, (fields - 1 - f) % rows, 0), pltpu.roll(value, rows - 1, 0)
        )
        return up, down

    def first_pass(main, rim):
        return [
            apply_l(coef, diag[f], main[f], *beside(main[f], rim, f)) for f in range(fields)
        ]

    def rim_pass(main, rim, far_rim):
        inside = packed(main, 0, rows - 1)
        up = jnp.where(low_half, far_rim, inside)
        down = jnp.where(low_half, inside, far_rim)
        return apply_l(coef_m, diag_m[...], rim, up, down)

    def second_pass(h, first, first_rim):
        u = [mixed(first, f) for f in range(fields)]
        u_rim = jnp.where(rim_mask, mixed_rim(first_rim), 0.0)
        for f in range(fields):
            qs[h, f] = apply_l(coef, diag[f], u[f], *beside(u[f], u_rim, f))[:, center]

    def send_q(h):
        pack(h + 1, [qs[h, f] for f in range(fields)])
        stacked = jnp.concatenate(
            [
                qs[h, f, :, c * patch : (c + 1) * patch]
                for c in range(per_row)
                for f in range(fields)
            ],
            axis=0,
        )
        high = stacked.astype(bf16)
        low = (stacked - high.astype(f32)).astype(bf16)
        chosen = gather_oh[...]
        patches = jnp.dot(chosen, low, preferred_element_type=f32) + jnp.dot(
            chosen, high, preferred_element_type=f32
        )
        xs[h] = patches.reshape(lon_n, SLOT_ROWS, patch)
        x_start(h)
        halo_start(h + 1)
        xr[h, my_lon] = xs[h, my_lon]

    main = [widened(bg[f], 0, f) for f in range(fields)]
    rim, far_rim = rims([widened_m(raw_m[0, f], 0, f) for f in range(fields)])
    second_pass(0, first_pass(main, rim), rim_pass(main, rim, far_rim))

    wait_rows(ask_rows, ask_recv.at[0])
    wanted = req[...].reshape(pos_n, 128)
    wanted = jnp.concatenate([wanted] * (patch_n // 128), axis=1)
    picked = wanted == lax.broadcasted_iota(i32, (pos_n, patch_n), 1)
    gather_oh[...] = jnp.where(picked, 1.0, 0.0).astype(bf16)
    send_q(0)

    lane1 = lax.broadcasted_iota(i32, (1, 128), 1)
    own_k, rim_k = lon_n * pos_n, 2 * lon_n * 2 * SLOT_ROWS

    def iota(n, axis):
        return lax.broadcasted_iota(i32, (n, 128), axis)

    own_rows = iota(patch_n, 0)
    side_rows = iota(fields * rows, 0)
    for group in range(own_k // 128):
        slots = jnp.full((1, 128), -1, i32)
        for h in range(lon_n):
            if h * pos_n // 128 == group:
                offset = h * pos_n % 128
                moved = turn(req_row[lon_n + h], offset)
                slots = jnp.where((lane1 >= offset) & (lane1 < offset + pos_n), moved, slots)
        lanes = slice(group * 128, (group + 1) * 128)
        at = lane1 % pos_n // SLOT_ROWS

        def match(rows_of, owner):
            wanted = jnp.where(at == owner, slots, -1)
            return jnp.where(rows_of == wanted, 1.0, 0.0).astype(bf16)

        own_oh[0:patch_n, lanes] = match(own_rows, my_lon)
        first_side, last_side = patch_n, patch_n + fields * rows
        own_oh[first_side:last_side, lanes] = match(
            (per_row - 1) * fields * rows + side_rows, west
        )
        own_oh[last_side : last_side + fields * rows, lanes] = match(side_rows, east)
        tile_rows = last_side + fields * rows
        mine = (iota(pos_n, 0) // SLOT_ROWS == at) & (ask[...].reshape(pos_n, 128) == slots)
        own_oh[tile_rows : tile_rows + pos_n, lanes] = jnp.where(mine, 1.0, 0.0).astype(bf16)

    for group in range(rim_k // 128):
        ours = jnp.full((1, 128), -1, i32)
        from_west, from_east = ours, ours
        side = group * 128 // (rim_k // 2)
        for index in range(2 * lon_n):
            if index * 2 * SLOT_ROWS // 128 != group:
                continue
            offset = index * 2 * SLOT_ROWS % 128
            table = jnp.broadcast_to(
                req_row[(index // lon_n) * 2 * lon_n + index % lon_n], (8, 128)
            )
            low = (lane1 >= offset) & (lane1 < offset + SLOT_ROWS)
            high = (lane1 >= offset + SLOT_ROWS) & (lane1 < offset + 2 * SLOT_ROWS)

            def brought(owner, to):
                by = (to - owner * SLOT_ROWS + 2 * 128) % 128
                return pltpu.roll(table, by, 1)[0:1]

            ours = jnp.where(low, brought(my_lon, offset), ours)
            from_west = jnp.where(high, brought(west, offset + SLOT_ROWS), from_west)
            from_east = jnp.where(high, brought(east, offset + SLOT_ROWS), from_east)
        lanes = slice(group * 128, (group + 1) * 128)
        is_north = (group * 128 + lane1) < rim_k // 2

        def match_rim(count, column, far, wanted):
            row = iota(count, 0)
            is_south = row % rows // fields
            line = jnp.where(is_south == 1, far, rows - 1 - far)
            number = ((row // rows + column) * fields + row % fields) * rows + line
            keep = (is_north & has_north & (is_south == 0)) | (
                (~is_north) & has_south & (is_south == 1)
            )
            return jnp.where(keep & (number == wanted), 1.0, 0.0)

        span = per_row * rows
        rim_oh[0:span, lanes] = match_rim(span, 0, 0, ours).astype(bf16)
        rim_oh[span : 2 * span, lanes] = match_rim(span, 0, 1, ours).astype(bf16)
        corners = [
            match_rim(rows, per_row - 1, 0, from_west),
            match_rim(rows, per_row - 1, 1, from_west),
            match_rim(rows, 0, 0, from_east),
            match_rim(rows, 0, 1, from_east),
        ]
        rim_oh[2 * span :, lanes] = jnp.concatenate(corners, axis=0).astype(bf16)

    lax.fori_loop(GRAMS_NEXT, tile_n, gram_of, 0)

    pos_sub = lax.broadcasted_iota(i32, (pos_n, patch), 0) % SLOT_ROWS

    def placed_field(blocks, f):
        return jnp.concatenate(
            [
                blocks[(c * fields + f) * rows : (c * fields + f + 1) * rows]
                for c in range(per_row)
            ],
            axis=1,
        )

    def received(h):
        wait_rows(x_rows + y_rows, near_recv.at[h])
        blocks = jnp.dot(
            own_oh[...], yr[h].reshape(own_k, patch), preferred_element_type=f32
        )
        came = xr[h].reshape(pos_n, patch)
        came = jnp.where(pos_sub < CAP, came, pltpu.roll(came, CAP, 0))
        seen = came + blocks[patch_n + 2 * fields * rows :]
        return seen, blocks

    def assembled(h, blocks):

        @pl.when(inner)
        def _():
            wait_rows(pack_rows + band_rows + msg_rows, rim_recv.at[h])

        @pl.when(jnp.logical_not(inner))
        def _():
            wait_rows(pack_rows + band_rows + msg_rows // 2, rim_recv.at[h])

        rim_blocks = jnp.dot(
            rim_oh[...], msg_in[h].reshape(rim_k, patch), preferred_element_type=f32
        )
        main = []
        for f in range(fields):
            west_rows = slice(patch_n + f * rows, patch_n + (f + 1) * rows)
            east_rows = slice(patch_n + (fields + f) * rows, patch_n + (fields + f + 1) * rows)
            main.append(
                jnp.concatenate(
                    [
                        west_part(pk_in, h + 1, f) + blocks[west_rows, patch - EDGE :],
                        qs[h, f] + placed_field(blocks, f),
                        east_part(pk_in, h + 1, f) + blocks[east_rows, :EDGE],
                    ],
                    axis=1,
                )
            )
        corner = 2 * per_row * rows

        def added(value, far):
            parts = [rim_blocks[corner + far * rows : corner + (far + 1) * rows, :EDGE]]
            for c in range(per_row):
                start = (far * per_row + c) * rows
                parts.append(rim_blocks[start : start + rows])
            start = corner + (2 + far) * rows
            parts.append(rim_blocks[start : start + rows, patch - EDGE :])
            return value + jnp.concatenate(parts, axis=1)

        rim, far_rim = rims([widened_m(qm[h, f], h + 1, f) for f in range(fields)])
        return main, added(rim, 0), added(far_rim, 1)

    def tile_images(seen):
        high = seen.astype(bf16).astype(f32)
        both = jnp.where(pos_sub < CAP, high, seen - high)
        acc = None
        for t in range(tile_n):
            term = jnp.dot(spread(both, t), gram[t], preferred_element_type=f32)
            acc = term if acc is None else acc + term
        swapped = pltpu.roll(acc.reshape(lon_n, SLOT_ROWS, patch), CAP, 1)
        return acc + swapped.reshape(pos_n, patch)

    seen, blocks = received(0)
    moments = []
    tau = None
    for it in range(ITERS):
        last = it == ITERS - 1
        images = tile_images(seen)
        y_put(it + 1, images)
        y_start(it + 1)
        main, rim, far_rim = assembled(it, blocks)
        if it == 2:
            main, rim, far_rim = [tau * v for v in main], tau * rim, tau * far_rim
        for f in range(fields):
            vecs[it, f] = main[f]
        vec_m[0], vec_m[1] = rim, far_rim
        main = [vecs[it, f] for f in range(fields)]
        rim, far_rim = vec_m[0], vec_m[1]
        first = first_pass(main, rim)
        u = [mixed(first, f)[:, center] for f in range(fields)]
        even = jnp.zeros((1, 128), f32)
        odd = lanes_of(jnp.where(pos_sub < CAP, seen * images, 0.0))
        for f in range(fields):
            here = main[f][:, center]
            even = even + lanes_of(here * here)
            odd = odd + lanes_of(u[f] * first[f][:, center])
        total_start(it, jnp.concatenate([even, odd], axis=1))
        second_pass(it + 1, first, rim_pass(main, rim, far_rim))
        if not last:
            send_q(it + 1)
            seen, blocks = received(it + 1)
            if it == 1:
                moments.append(total(0))
                tau = moments[0][0] / moments[0][1]
                seen = tau * seen
    wait_rows(y_rows, near_recv.at[ITERS])
    blocks = jnp.dot(
        own_oh[0:patch_n, :], yr[ITERS].reshape(own_k, patch), preferred_element_type=f32
    )

    m2, m3 = total(1)
    scale = 1.0 / moments[0][0]
    g2, g3 = tau * tau * m2 * scale, tau * tau * tau * m3 * scale
    beta0 = g2 - 1.0
    c0 = 1.0 + beta0
    alpha1 = beta0 / (c0 * c0 - 2.0 * c0 * g2 + g3)
    a1, a2 = -1.0 - alpha1 * c0, alpha1
    m4, m5 = total(2)
    g4, g5 = tau * tau * m4 * scale, tau * tau * tau * m5 * scale
    gamma2 = 1.0 + 2.0 * a1 + (a1 * a1 + 2.0 * a2) * g2 + 2.0 * a1 * a2 * g3 + a2 * a2 * g4
    beta1 = gamma2 / beta0
    b0, b1, b2 = 1.0 + beta1 * c0, a1 - beta1, a2
    alpha2 = gamma2 / (
        b0 * b0
        + 2.0 * b0 * b1 * g2
        + (b1 * b1 + 2.0 * b0 * b2) * g3
        + 2.0 * b1 * b2 * g4
        + b2 * b2 * g5
    )
    x0, x1, x2 = (
        tau * (1.0 + alpha1 * c0 + alpha2 * b0),
        tau * tau * (alpha2 * b1 - alpha1),
        tau * tau * (alpha2 * b2),
    )
    r1, r2, r3 = tau * (a1 - alpha2 * b0), tau * (a2 - alpha2 * b1), -tau * tau * (alpha2 * b2)
    for f in range(fields):
        e0, e1, e2 = (vecs[it, f, :, center] for it in range(ITERS))
        sol_out[f] = x0 * e0 + x1 * e1 + x2 * e2
        res_out[f] = e0 + r1 * e1 + r2 * e2 + r3 * (qs[ITERS, f] + placed_field(blocks, f))

    @pl.when(inner)
    def _():
        wait_rows(sent_rows(sizes, bg.shape, patch), sent.at[0])

    @pl.when(jnp.logical_not(inner))
    def _():
        wait_rows(sent_rows(sizes, bg.shape, patch) - ITERS * msg_rows // 2, sent.at[0])


def sent_rows(sizes, shape, patch):
    lon_n, lat_n, fld_n = sizes
    fields, rows, cols = shape
    dev_n, pos_n = lon_n * lat_n * fld_n, lon_n * SLOT_ROWS
    halos = (ITERS + 1) * (2 * rows + 8) + (3 + ITERS) * 4 * fields * cols // 128
    asks = (lon_n - 1) * SLOT_ROWS + 3 * lon_n - 1
    inputs = ITERS * (lon_n - 1) * CAP * patch // 128
    images = (ITERS + 1) * (lon_n - 1) * pos_n * patch // 256
    rims = ITERS * 2 * lon_n * 2 * SLOT_ROWS * patch // 256
    return halos + asks + inputs + images + rims + ITERS * (dev_n - 1) * 2


def on_device(
    sizes,
    background,
    decay_sq,
    edge_weight,
    coupling,
    obs_tiles,
    obs_values,
    obs_weights,
    obs_counts,
    swath_ids,
    swath_scale,
    tile_owner,
    tile_slot,
):
    fields, rows, cols = background.shape
    tile_n, obs_len, patch = obs_tiles.shape
    lon_n, lat_n, fld_n = sizes
    dev_n = lon_n * lat_n * fld_n
    ext = cols + 2 * EDGE
    pos_n = lon_n * SLOT_ROWS
    patch_n = fields * rows * cols // patch
    side_n = 2 * fields * rows
    halos = ITERS + 1
    f32, bf16, i32 = jnp.float32, jnp.bfloat16, jnp.int32
    vmem = pl.BlockSpec(memory_space=pltpu.VMEM)
    dma = pltpu.SemaphoreType.DMA
    shape = pltpu.VMEM((fields, rows, cols), f32)
    block = pltpu.VMEM((fields, rows, ext), f32)
    return pl.pallas_call(
        functools.partial(kernel, sizes),
        out_shape=(shape, shape),
        in_specs=[pl.BlockSpec(memory_space=pltpu.HBM)] * 12,
        out_specs=(vmem, vmem),
        scratch_shapes=[
            pltpu.SMEM(tile_owner.shape, i32),
            pltpu.SMEM(tile_slot.shape, i32),
            pltpu.SMEM(obs_counts.shape, i32),
            pltpu.SMEM(swath_ids.shape, i32),
            pltpu.SMEM(swath_scale.shape, f32),
            pltpu.SMEM(coupling.shape, f32),
            pltpu.VMEM(background.shape, f32),
            pltpu.VMEM(decay_sq.shape, f32),
            pltpu.VMEM(edge_weight.shape, f32),
            pltpu.VMEM(obs_values.shape, f32),
            pltpu.VMEM(obs_weights.shape, f32),
            pltpu.VMEM((tile_n, obs_len, patch), bf16),
            pltpu.VMEM((tile_n, patch, patch), bf16),
            pltpu.VMEM((2 * tile_n, obs_len), bf16),
            pltpu.VMEM((tile_n, obs_len), f32),
            pltpu.VMEM((pos_n, patch), i32),
            pltpu.VMEM((8, rows, ext), f32),
            pltpu.VMEM((8, rows, ext), f32),
            block,
            pltpu.VMEM((rows, ext), f32),
            pltpu.VMEM((ITERS, fields, rows, ext), f32),
            pltpu.VMEM((2, rows, ext), f32),
            pltpu.VMEM((ITERS + 1, fields, rows, cols), f32),
            pltpu.VMEM((ITERS, fields, rows, cols), f32),
            pltpu.VMEM((3, fields, rows, cols), f32),
            pltpu.VMEM((halos, 2, rows, EDGE), f32),
            pltpu.VMEM((halos, 2, rows, EDGE), f32),
            pltpu.VMEM((halos, 2, rows, EDGE), f32),
            pltpu.VMEM((lon_n, SLOT_ROWS, 128), i32),
            pltpu.VMEM((lon_n, SLOT_ROWS, 128), i32),
            pltpu.VMEM((1, 128), i32),
            pltpu.VMEM((3 * lon_n, 1, 128), i32),
            pltpu.VMEM((pos_n, patch_n), bf16),
            pltpu.VMEM((patch_n + side_n + pos_n, lon_n * pos_n), bf16),
            pltpu.VMEM((2 * rows * (cols // patch) + 4 * rows, 4 * lon_n * SLOT_ROWS), bf16),
            pltpu.VMEM((ITERS, lon_n, SLOT_ROWS, patch), f32),
            pltpu.VMEM((ITERS, lon_n, SLOT_ROWS, patch), f32),
            pltpu.VMEM((ITERS + 1, pos_n, patch), bf16),
            pltpu.VMEM((ITERS + 1, lon_n, pos_n, patch), bf16),
            pltpu.VMEM((ITERS, lon_n, 2 * SLOT_ROWS, patch), bf16),
            pltpu.VMEM((ITERS, 2, lon_n, 2 * SLOT_ROWS, patch), bf16),
            pltpu.VMEM((ITERS, 1, 256), f32),
            pltpu.VMEM((ITERS, dev_n, 1, 256), f32),
            pltpu.VMEM((sent_rows(sizes, background.shape, patch), 128), f32),
            dma((1,)),
            dma((1,)),
            dma((1,)),
            dma((ITERS + 1,)),
            dma((ITERS,)),
            dma((ITERS,)),
            dma((10,)),
        ],
        compiler_params=pltpu.CompilerParams(
            collective_id=0, has_side_effects=True, vmem_limit_bytes=67043328 - 3 * 2**20
        ),
    )(
        tile_owner,
        tile_slot,
        obs_counts,
        swath_ids,
        swath_scale,
        coupling,
        background,
        decay_sq,
        edge_weight,
        obs_tiles,
        obs_values,
        obs_weights,
    )


def solution(mesh):
    sizes = (mesh.shape["lon"], mesh.shape["lat"], mesh.shape["fld"])
    return jax.shard_map(
        functools.partial(on_device, sizes),
        mesh=mesh,
        in_specs=(
            P("group", ("lat", "fld"), "lon"),
            P(None, ("lat", "fld"), "lon"),
            P(None, ("lat", "fld"), "lon"),
            P(),
            P(("lon", "lat", "fld"), None, None),
            P(("group", "lon", "lat", "fld"), None),
            P(("lon", "lat", "fld"), None),
            P(("lon", "lat", "fld")),
            P(("lon", "lat", "fld")),
            P(),
            P(("lon", "lat", "fld")),
            P(("lon", "lat", "fld")),
        ),
        out_specs=(P("group", ("lat", "fld"), "lon"), P("group", ("lat", "fld"), "lon")),
        check_vma=False,
    )
```

```python
import functools

import jax
import jax.numpy as jnp
from jax import lax
from jax.experimental import pallas as pl
from jax.experimental.pallas import tpu as pltpu
from jax.sharding import PartitionSpec as P

CAP = 4
ITERS = 3
SLOT_ROWS = 8
EDGE = 128
GRAMS_AHEAD = 2
GRAMS_NEXT = 12
MESH = pl.DeviceIdType.MESH


def loop(low, high, body):
    if high - low <= 16:
        for k in range(low, high):
            body(k)
    else:
        lax.fori_loop(low, high, lambda k, c: (body(k), c)[1], 0)


def kernel(
    sizes,
    owner_hbm,
    slot_hbm,
    counts_hbm,
    swath_hbm,
    scale_hbm,
    coupling_hbm,
    bg_hbm,
    decay_hbm,
    edge_hbm,
    tiles_hbm,
    values_hbm,
    weights_hbm,
    sol_out,
    res_out,
    owner_s,
    slot_s,
    counts_s,
    swath_s,
    scale_s,
    coupling_s,
    bg,
    decay,
    edge,
    obs_values,
    obs_weights,
    tiles,
    gram,
    w_parts,
    q_rows,
    tile_of,
    coef,
    coef_m,
    diag,
    diag_m,
    vecs,
    vec_m,
    qs,
    qm,
    raw_m,
    pk_out,
    pk_in,
    pkm_in,
    ask,
    req,
    ask_row,
    req_row,
    gather_oh,
    own_oh,
    rim_oh,
    xs,
    xr,
    yv,
    yr,
    msg,
    msg_in,
    part,
    parts,
    seen_s,
    blocks_s,
    bytes_of,
    sent,
    halo_recv,
    ask_recv,
    near_recv,
    rim_recv,
    red_recv,
    load_sem,
):
    lon_n, lat_n, fld_n = sizes
    row_n = lat_n * fld_n
    dev_n = lon_n * row_n
    fields, rows, cols = bg.shape
    tile_n, obs_len, patch = tiles.shape
    ext = cols + 2 * EDGE
    per_row = cols // patch
    patch_n = fields * rows * per_row
    pos_n = lon_n * SLOT_ROWS
    bf16, f32, i32 = jnp.bfloat16, jnp.float32, jnp.int32

    my_lon = lax.axis_index("lon")
    my_row = lax.axis_index("lat") * fld_n + lax.axis_index("fld")
    me = my_lon * row_n + my_row

    def device(lon, row):
        return {"lon": lon, "lat": row // fld_n, "fld": row % fld_n}

    west, east = (my_lon + lon_n - 1) % lon_n, (my_lon + 1) % lon_n
    north, south = (my_row + row_n - 1) % row_n, (my_row + 1) % row_n
    has_north = my_row > 0
    has_south = my_row < row_n - 1
    inner = has_north & has_south

    loads = [
        pltpu.make_async_copy(src, dst, load_sem.at[k])
        for k, src, dst in (
            (0, owner_hbm, owner_s),
            (1, slot_hbm, slot_s),
            (2, counts_hbm, counts_s),
            (3, swath_hbm, swath_s),
            (4, scale_hbm, scale_s),
            (5, coupling_hbm, coupling_s),
            (6, values_hbm, obs_values),
            (7, weights_hbm, obs_weights),
            (8, tiles_hbm, tiles),
            (9, edge_hbm, edge),
            (9, bg_hbm, bg),
            (9, decay_hbm, decay),
        )
    ]
    for load in loads:
        load.start()

    barrier = pltpu.get_barrier_semaphore()

    def greet(k):
        other = (me + k) % dev_n
        pl.semaphore_signal(
            barrier, inc=1, device_id=device(other // row_n, other % row_n), device_id_type=MESH
        )

    for side, there in ((0, has_north), (1, has_south)):

        @pl.when(jnp.logical_not(there))
        def _():
            for i in range(ITERS):
                msg_in[i, side] = jnp.zeros(msg_in.shape[2:], bf16)

    loop(1, dev_n, greet)

    center = slice(EDGE, EDGE + cols)
    lane8 = lax.broadcasted_iota(i32, (rows, EDGE), 1)
    sub_e = lax.broadcasted_iota(i32, (rows, ext), 0)
    top, bottom = sub_e == 0, sub_e == rows - 1
    low_half = sub_e < fields
    rim_mask = (low_half & has_north) | ((sub_e >= fields) & has_south)
    edge_mask = ((sub_e < 2) & has_south) | ((sub_e >= rows - 2) & has_north)

    toward = jnp.where(my_lon < lon_n // 2, lon_n - 1, 1)

    def remote_start(src, dst, recv_sem, lon, row):
        pltpu.make_async_remote_copy(
            src_ref=src,
            dst_ref=dst,
            send_sem=sent.at[0],
            recv_sem=recv_sem,
            device_id=device(lon, row),
            device_id_type=MESH,
        ).start()

    def wait_rows(count, sem):
        some = bytes_of.at[pl.ds(0, count)]
        pltpu.make_async_copy(some, some, sem).wait()

    band_rows = 2 * fields * 2 * cols // 128
    pack_rows = 2 * rows + 4 * 2
    x_rows = (lon_n - 1) * CAP * patch // 128
    y_rows = (lon_n - 1) * pos_n * patch // 256
    msg_rows = 2 * lon_n * 2 * SLOT_ROWS * patch // 256
    ask_rows = (lon_n - 1) * SLOT_ROWS + 3 * lon_n - 1
    sum_rows = (dev_n - 1) * 2

    def turn(value, by):
        return pltpu.roll(value, by % EDGE, 1) if by % EDGE else value

    first_two, last_two = pl.ds(0, 2), pl.ds(rows - 2, 2)

    def halo_start(h):
        pairs = [
            (pk_out.at[h, 0], pk_in.at[h, 1], west, my_row),
            (pk_out.at[h, 1], pk_in.at[h, 0], east, my_row),
            (pk_out.at[h, 0, first_two], pkm_in.at[h, 1, first_two], west, north),
            (pk_out.at[h, 1, first_two], pkm_in.at[h, 0, first_two], east, north),
            (pk_out.at[h, 0, last_two], pkm_in.at[h, 1, last_two], west, south),
            (pk_out.at[h, 1, last_two], pkm_in.at[h, 0, last_two], east, south),
        ]
        if isinstance(h, int) and h == 0:
            bands = [(bg, raw_m.at[0]), (edge, raw_m.at[1]), (decay, raw_m.at[2])]
        else:
            bands = [(qs.at[h - 1], qm.at[h - 1])]
        for src, dst in bands:
            pairs.append((src.at[:, first_two], dst.at[:, first_two], my_lon, north))
            pairs.append((src.at[:, last_two], dst.at[:, last_two], my_lon, south))
        sem = halo_recv.at[0] if isinstance(h, int) and h == 0 else rim_recv.at[h - 1]
        for src, dst, lon, row in pairs[:2]:
            remote_start(src, dst, sem, lon, row)

        @pl.when(has_north)
        def _():
            for src, dst, lon, row in pairs[2:]:
                if row is north:
                    remote_start(src, dst, sem, lon, row)

        @pl.when(has_south)
        def _():
            for src, dst, lon, row in pairs[2:]:
                if row is south:
                    remote_start(src, dst, sem, lon, row)

    def pack(h, values):
        to_west = jnp.zeros((rows, EDGE), f32)
        to_east = to_west
        for g, value in enumerate(values):
            here = lane8 // 2 == g
            to_west = jnp.where(here, turn(value[:, 0:EDGE], 2 * g), to_west)
            to_east = jnp.where(here, turn(value[:, cols - EDGE : cols], 2 * g + 2), to_east)
        pk_out[h, 0] = to_west
        pk_out[h, 1] = to_east

    def west_part(buffer, h, g):
        return turn(buffer[h, 0], EDGE - 2 - 2 * g)

    def east_part(buffer, h, g):
        return turn(buffer[h, 1], EDGE - 2 * g)

    def widened(value, h, g):
        return jnp.concatenate([west_part(pk_in, h, g), value, east_part(pk_in, h, g)], axis=1)

    def widened_m(value, h, g):
        return jnp.concatenate([west_part(pkm_in, h, g), value, east_part(pkm_in, h, g)], axis=1)

    def packed(values, north_row, south_row):
        out = pltpu.roll(values[0], -north_row % rows, 0)
        for f in range(1, fields):
            out = jnp.where(sub_e == f, pltpu.roll(values[f], (f - north_row) % rows, 0), out)
        for f in range(fields):
            moved = pltpu.roll(values[f], (fields + f - south_row) % rows, 0)
            out = jnp.where(sub_e == fields + f, moved, out)
        return out

    def rims(values):
        near_rim = packed(values, rows - 1, 0)
        far_rim = packed(values, rows - 2, 1)
        return jnp.where(rim_mask, near_rim, 0.0), jnp.where(rim_mask, far_rim, 0.0)

    def y_put(i, value, with_rim=True):
        pos_half = lax.broadcasted_iota(i32, (pos_n, patch), 0) % SLOT_ROWS < CAP
        high = value.astype(bf16).astype(f32)
        both = jnp.where(pos_half, high, value - high)
        full = both.astype(bf16)
        yv[i] = full
        yr[i, my_lon] = full
        if with_rim:
            blocks = [both[l * SLOT_ROWS : (l + 1) * SLOT_ROWS] for l in range(lon_n)]
            for l in range(lon_n):
                rim = jnp.concatenate(
                    [blocks[l - 1][:, patch - EDGE :], blocks[(l + 1) % lon_n][:, :EDGE]], axis=1
                )
                msg[i, l] = jnp.concatenate([blocks[l], rim], axis=0).astype(bf16)

    def y_start(i, with_rim=True):
        def send(k):
            remote_start(
                yv.at[i], yr.at[i, my_lon], near_recv.at[i], (my_lon + k * toward) % lon_n, my_row
            )

        loop(1, lon_n, send)
        if with_rim:

            def send_rim(k):
                to = (my_lon + k * toward) % lon_n

                @pl.when(has_north)
                def _():
                    remote_start(msg.at[i, to], msg_in.at[i, 1, my_lon], rim_recv.at[i], to, north)

                @pl.when(has_south)
                def _():
                    remote_start(msg.at[i, to], msg_in.at[i, 0, my_lon], rim_recv.at[i], to, south)

            loop(0, lon_n, send_rim)

    def x_start(i):
        def send(k):
            to = (my_lon + k * toward) % lon_n
            remote_start(
                xs.at[i, to, pl.ds(0, CAP)],
                xr.at[i, my_lon, pl.ds(0, CAP)],
                near_recv.at[i],
                to,
                my_row,
            )

        loop(1, lon_n, send)

    def total_start(k, value):
        part[k] = value
        parts[k, me] = value

        def send(j):
            lon = (my_lon + (j // row_n + 1) * toward) % lon_n
            row = (my_row + j % row_n + row_n // 2) % row_n
            remote_start(part.at[k], parts.at[k, me], red_recv.at[k], lon, row)

        def send_along(j):
            row = (my_row + j) % row_n
            remote_start(part.at[k], parts.at[k, me], red_recv.at[k], my_lon, row)

        loop(0, (lon_n - 1) * row_n, send)
        loop(1, row_n, send_along)

    def total(k):
        wait_rows(sum_rows, red_recv.at[k])
        sums = jnp.sum(parts[k], axis=0)
        return (
            jnp.sum(sums[:, 0:128], axis=1, keepdims=True),
            jnp.sum(sums[:, 128:256], axis=1, keepdims=True),
        )

    def lanes_of(value):
        lane_sum = value[:, 0:128]
        for k in range(1, value.shape[1] // 128):
            lane_sum = lane_sum + value[:, k * 128 : (k + 1) * 128]
        return jnp.sum(lane_sum, axis=0, keepdims=True)

    def mixed(values, f):
        acc = coupling_s[f, 0] * values[0]
        for g in range(1, fields):
            acc = acc + coupling_s[f, g] * values[g]
        return acc

    for load in loads[:8]:
        load.wait()

    pos_row = lax.broadcasted_iota(i32, (pos_n, 128), 0)
    row_lane = lax.broadcasted_iota(i32, (8, 128), 1)
    tile_row = lax.broadcasted_iota(i32, (tile_n, obs_len), 0)
    obs_lane = lax.broadcasted_iota(i32, (tile_n, obs_len), 1)
    holds = jnp.full((pos_n, 128), -1, i32)
    asked = jnp.full((pos_n, 128), -2, i32)
    asked_row = jnp.full((8, 128), -1, i32)
    scale_of = jnp.zeros((tile_n, obs_len), f32)
    count_of = jnp.zeros((tile_n, obs_len), i32)
    for t in range(tile_n):
        rank = jnp.int32(0)
        for other in range(t):
            rank = rank + (owner_s[other] == owner_s[t]).astype(i32)
        number = slot_s[t]
        column, rest = number % per_row, number // per_row
        moved = (column * fields + rest // rows) * rows + rest % rows
        place = owner_s[t] * SLOT_ROWS + rank
        here = (pos_row == place) | (pos_row == place + CAP)
        here_row = (row_lane == place) | (row_lane == place + CAP)
        holds = jnp.where(here, t, holds)
        asked = jnp.where(here, moved, asked)
        asked_row = jnp.where(here_row, moved, asked_row)
        scale_of = jnp.where(tile_row == t, scale_s[swath_s[t]], scale_of)
        count_of = jnp.where(tile_row == t, counts_s[t], count_of)
    tile_of[...] = jnp.concatenate([holds] * (patch // 128), axis=1)
    ask[...] = asked.reshape(lon_n, SLOT_ROWS, 128)
    req[my_lon] = ask[my_lon]
    ask_row[...] = asked_row[0:1]
    req_row[lon_n + my_lon] = asked_row[0:1]
    weight = jnp.where(obs_lane < count_of, obs_weights[...] * scale_of, 0.0)
    weight_high = weight.astype(bf16).astype(f32)
    w_parts[...] = jnp.concatenate([weight_high, weight - weight_high], axis=0).astype(bf16)
    q_rows[...] = (weight * obs_values[...]).astype(bf16).astype(f32)

    def spread(value, t):
        return jnp.where(tile_of[...] == t, value, 0.0).astype(bf16)

    loads[8].wait()
    acc = None
    for t in range(tile_n):
        term = jnp.dot(
            spread(q_rows[t : t + 1, :], t), tiles[t], preferred_element_type=f32
        )
        acc = term if acc is None else acc + term
    y_put(0, acc)

    pick_row = lax.broadcasted_iota(i32, (2 * tile_n, 128), 0) % tile_n

    def gram_of(t, carry):
        chosen = jnp.where(pick_row == t, 1.0, 0.0).astype(bf16)
        column = lax.dot_general(
            w_parts[...], chosen, (((0,), (0,)), ((), ())), preferred_element_type=f32
        )
        tile = tiles[t]
        scaled = (tile.astype(f32) * jnp.concatenate([column] * (patch // 128), axis=1)).astype(bf16)
        gram[t] = lax.dot_general(
            tile, scaled, (((0,), (0,)), ((), ())), preferred_element_type=f32
        ).astype(bf16)
        return carry

    lax.fori_loop(0, GRAMS_AHEAD, gram_of, 0)

    pltpu.make_async_copy(raw_m, raw_m, load_sem.at[9]).wait()
    pack(0, [bg[f] for f in range(fields)] + [edge[e] for e in range(4)] + [decay[f] for f in range(fields)])

    pl.semaphore_wait(barrier, dev_n - 1)
    halo_start(0)

    def send_ask(k):
        to = (my_lon + k * toward) % lon_n
        remote_start(ask.at[to], req.at[my_lon], ask_recv.at[0], to, my_row)
        remote_start(ask_row, req_row.at[lon_n + my_lon], ask_recv.at[0], to, my_row)

    def send_ask_rim(k):
        to = (my_lon + k * toward) % lon_n
        remote_start(ask_row, req_row.at[2 * lon_n + my_lon], ask_recv.at[0], to, north)
        remote_start(ask_row, req_row.at[my_lon], ask_recv.at[0], to, south)

    loop(1, lon_n, send_ask)
    loop(0, lon_n, send_ask_rim)

    y_start(0)
    lax.fori_loop(GRAMS_AHEAD, GRAMS_NEXT, gram_of, 0)


    @pl.when(inner)
    def _():
        wait_rows(pack_rows + 3 * band_rows, halo_recv.at[0])

    @pl.when(jnp.logical_not(inner))
    def _():
        wait_rows(pack_rows - 4 + 3 * band_rows // 2, halo_recv.at[0])

    w = [widened(edge[e], 0, 4 + e) for e in range(4)]
    wm = [jnp.where(edge_mask, widened_m(raw_m[1, e], 0, 4 + e), 0.0) for e in range(4)]

    def around(main, rim):
        m1, r1 = pltpu.roll(main, 1, 0), pltpu.roll(rim, 1, 0)
        m7, r7 = pltpu.roll(main, rows - 1, 0), pltpu.roll(rim, rows - 1, 0)
        return (
            jnp.where(top, r1, m1),
            jnp.where(bottom, r7, m7),
            jnp.where(top, m1, r1),
            jnp.where(bottom, m7, r7),
        )

    near = [around(w[e], wm[e]) for e in range(4)]

    def coefficients(here, up, down):
        w_west = {e: pltpu.roll(here[e], 1, 1) for e in (0, 2, 3)}
        w_east = {e: pltpu.roll(here[e], ext - 1, 1) for e in (0, 2, 3)}
        e0, e1, e2 = (
            0.5 * (w_west[0] + here[0]),
            0.5 * (w_west[3] + up[3]),
            0.5 * (w_west[2] + down[2]),
        )
        v0, v1, v2 = (
            0.5 * (w_east[0] + here[0]),
            0.5 * (w_east[2] + up[2]),
            0.5 * (w_east[3] + down[3]),
        )
        n0, n1 = 0.5 * (here[1] + up[1]), 0.5 * (here[1] + down[1])
        degree = (
            n0 + n1 + pltpu.roll(e0 + e1 + e2, ext - 1, 1) + pltpu.roll(v0 + v1 + v2, 1, 1)
        )
        return (e0, e1, e2, v0, v1, v2, n0, n1), degree

    values, degree = coefficients(
        w, [near[e][0] for e in range(4)], [near[e][1] for e in range(4)]
    )
    for k, value in enumerate(values):
        coef[k] = value
    for f in range(fields):
        diag[f] = widened(decay[f], 0, 8 + f) + degree
    values, degree = coefficients(
        wm, [near[e][2] for e in range(4)], [near[e][3] for e in range(4)]
    )
    for k, value in enumerate(values):
        coef_m[k] = jnp.where(low_half, value[rows - 1 : rows], value[0:1])
    diag_m[...] = packed(
        [widened_m(raw_m[2, f], 0, 8 + f) + degree for f in range(fields)], rows - 1, 0
    )

    def apply_l(c, d, value, up, down):
        toward_east = c[0] * value + c[1] * up + c[2] * down
        toward_west = c[3] * value + c[4] * up + c[5] * down
        result = d * value - c[6] * up - c[7] * down
        return result - pltpu.roll(toward_east, ext - 1, 1) - pltpu.roll(toward_west, 1, 1)

    lane_row = lax.broadcasted_iota(i32, (rows, 128), 0)
    blends = []
    for d in range(fields):
        blend = jnp.zeros((rows, 128), f32)
        for k in range(rows):
            blend = jnp.where(lane_row == k, coupling_s[k % fields, (k + d) % fields], blend)
        blends.append(jnp.concatenate([blend] * (ext // 128), axis=1))

    def mixed_rim(value):
        acc = blends[0] * value
        for d in range(1, fields):
            ahead = pltpu.roll(value, rows - d, 0)
            behind = pltpu.roll(value, fields - d, 0)
            acc = acc + blends[d] * jnp.where(sub_e % fields < fields - d, ahead, behind)
        return acc

    def beside(value, rim, f):
        up = jnp.where(top, pltpu.roll(rim, -f % rows, 0), pltpu.roll(value, 1, 0))
        down = jnp.where(
            bottom, pltpu.roll(rim, (fields - 1 - f) % rows, 0), pltpu.roll(value, rows - 1, 0)
        )
        return up, down

    def first_pass(main, rim):
        return [
            apply_l(coef, diag[f], main[f], *beside(main[f], rim, f)) for f in range(fields)
        ]

    def rim_pass(main, rim, far_rim):
        inside = packed(main, 0, rows - 1)
        up = jnp.where(low_half, far_rim, inside)
        down = jnp.where(low_half, inside, far_rim)
        return apply_l(coef_m, diag_m[...], rim, up, down)

    def second_pass(h, first, first_rim):
        u = [mixed(first, f) for f in range(fields)]
        u_rim = jnp.where(rim_mask, mixed_rim(first_rim), 0.0)
        for f in range(fields):
            qs[h, f] = apply_l(coef, diag[f], u[f], *beside(u[f], u_rim, f))[:, center]

    def send_q(h):
        pack(h + 1, [qs[h, f] for f in range(fields)])
        stacked = jnp.concatenate(
            [
                qs[h, f, :, c * patch : (c + 1) * patch]
                for c in range(per_row)
                for f in range(fields)
            ],
            axis=0,
        )
        high = stacked.astype(bf16)
        low = (stacked - high.astype(f32)).astype(bf16)
        chosen = gather_oh[...]
        patches = jnp.dot(chosen, low, preferred_element_type=f32) + jnp.dot(
            chosen, high, preferred_element_type=f32
        )
        xs[h] = patches.reshape(lon_n, SLOT_ROWS, patch)
        x_start(h)
        halo_start(h + 1)
        xr[h, my_lon] = xs[h, my_lon]

    main = [widened(bg[f], 0, f) for f in range(fields)]
    rim, far_rim = rims([widened_m(raw_m[0, f], 0, f) for f in range(fields)])
    second_pass(0, first_pass(main, rim), rim_pass(main, rim, far_rim))

    wait_rows(ask_rows, ask_recv.at[0])
    wanted = req[...].reshape(pos_n, 128)
    wanted = jnp.concatenate([wanted] * (patch_n // 128), axis=1)
    picked = wanted == lax.broadcasted_iota(i32, (pos_n, patch_n), 1)
    gather_oh[...] = jnp.where(picked, 1.0, 0.0).astype(bf16)
    send_q(0)

    lane1 = lax.broadcasted_iota(i32, (1, 128), 1)
    own_k, rim_k = lon_n * pos_n, 2 * lon_n * 2 * SLOT_ROWS

    def iota(n, axis):
        return lax.broadcasted_iota(i32, (n, 128), axis)

    own_rows = iota(patch_n, 0)
    side_rows = iota(fields * rows, 0)
    for group in range(own_k // 128):
        slots = jnp.full((1, 128), -1, i32)
        for h in range(lon_n):
            if h * pos_n // 128 == group:
                offset = h * pos_n % 128
                moved = turn(req_row[lon_n + h], offset)
                slots = jnp.where((lane1 >= offset) & (lane1 < offset + pos_n), moved, slots)
        lanes = slice(group * 128, (group + 1) * 128)
        at = lane1 % pos_n // SLOT_ROWS

        def match(rows_of, owner):
            wanted = jnp.where(at == owner, slots, -1)
            return jnp.where(rows_of == wanted, 1.0, 0.0).astype(bf16)

        own_oh[0:patch_n, lanes] = match(own_rows, my_lon)
        first_side, last_side = patch_n, patch_n + fields * rows
        own_oh[first_side:last_side, lanes] = match(
            (per_row - 1) * fields * rows + side_rows, west
        )
        own_oh[last_side : last_side + fields * rows, lanes] = match(side_rows, east)
        tile_rows = last_side + fields * rows
        mine = (iota(pos_n, 0) // SLOT_ROWS == at) & (ask[...].reshape(pos_n, 128) == slots)
        own_oh[tile_rows : tile_rows + pos_n, lanes] = jnp.where(mine, 1.0, 0.0).astype(bf16)

    for group in range(rim_k // 128):
        ours = jnp.full((1, 128), -1, i32)
        from_west, from_east = ours, ours
        side = group * 128 // (rim_k // 2)
        for index in range(2 * lon_n):
            if index * 2 * SLOT_ROWS // 128 != group:
                continue
            offset = index * 2 * SLOT_ROWS % 128
            table = jnp.broadcast_to(
                req_row[(index // lon_n) * 2 * lon_n + index % lon_n], (8, 128)
            )
            low = (lane1 >= offset) & (lane1 < offset + SLOT_ROWS)
            high = (lane1 >= offset + SLOT_ROWS) & (lane1 < offset + 2 * SLOT_ROWS)

            def brought(owner, to):
                by = (to - owner * SLOT_ROWS + 2 * 128) % 128
                return pltpu.roll(table, by, 1)[0:1]

            ours = jnp.where(low, brought(my_lon, offset), ours)
            from_west = jnp.where(high, brought(west, offset + SLOT_ROWS), from_west)
            from_east = jnp.where(high, brought(east, offset + SLOT_ROWS), from_east)
        lanes = slice(group * 128, (group + 1) * 128)
        is_north = (group * 128 + lane1) < rim_k // 2

        def match_rim(count, column, far, wanted):
            row = iota(count, 0)
            is_south = row % rows // fields
            line = jnp.where(is_south == 1, far, rows - 1 - far)
            number = ((row // rows + column) * fields + row % fields) * rows + line
            keep = (is_north & has_north & (is_south == 0)) | (
                (~is_north) & has_south & (is_south == 1)
            )
            return jnp.where(keep & (number == wanted), 1.0, 0.0)

        span = per_row * rows
        rim_oh[0:span, lanes] = match_rim(span, 0, 0, ours).astype(bf16)
        rim_oh[span : 2 * span, lanes] = match_rim(span, 0, 1, ours).astype(bf16)
        corners = [
            match_rim(rows, per_row - 1, 0, from_west),
            match_rim(rows, per_row - 1, 1, from_west),
            match_rim(rows, 0, 0, from_east),
            match_rim(rows, 0, 1, from_east),
        ]
        rim_oh[2 * span :, lanes] = jnp.concatenate(corners, axis=0).astype(bf16)

    lax.fori_loop(GRAMS_NEXT, tile_n, gram_of, 0)

    pos_sub = lax.broadcasted_iota(i32, (pos_n, patch), 0) % SLOT_ROWS

    def placed_field(blocks, f):
        return jnp.concatenate(
            [
                blocks[(c * fields + f) * rows : (c * fields + f + 1) * rows]
                for c in range(per_row)
            ],
            axis=1,
        )

    def received(h):
        wait_rows(x_rows + y_rows, near_recv.at[h])
        blocks = jnp.dot(
            own_oh[...], yr[h].reshape(own_k, patch), preferred_element_type=f32
        )
        came = xr[h].reshape(pos_n, patch)
        came = jnp.where(pos_sub < CAP, came, pltpu.roll(came, CAP, 0))
        seen = came + blocks[patch_n + 2 * fields * rows :]
        seen_s[...] = seen
        blocks_s[...] = blocks

    def assembled(h):
        blocks = blocks_s[...]

        @pl.when(inner)
        def _():
            wait_rows(pack_rows + band_rows + msg_rows, rim_recv.at[h])

        @pl.when(jnp.logical_not(inner))
        def _():
            wait_rows(pack_rows - 4 + (band_rows + msg_rows) // 2, rim_recv.at[h])

        rim_blocks = jnp.dot(
            rim_oh[...], msg_in[h].reshape(rim_k, patch), preferred_element_type=f32
        )
        main = []
        for f in range(fields):
            west_rows = slice(patch_n + f * rows, patch_n + (f + 1) * rows)
            east_rows = slice(patch_n + (fields + f) * rows, patch_n + (fields + f + 1) * rows)
            main.append(
                jnp.concatenate(
                    [
                        west_part(pk_in, h + 1, f) + blocks[west_rows, patch - EDGE :],
                        qs[h, f] + placed_field(blocks, f),
                        east_part(pk_in, h + 1, f) + blocks[east_rows, :EDGE],
                    ],
                    axis=1,
                )
            )
        corner = 2 * per_row * rows

        def added(value, far):
            parts = [rim_blocks[corner + far * rows : corner + (far + 1) * rows, :EDGE]]
            for c in range(per_row):
                start = (far * per_row + c) * rows
                parts.append(rim_blocks[start : start + rows])
            start = corner + (2 + far) * rows
            parts.append(rim_blocks[start : start + rows, patch - EDGE :])
            return value + jnp.concatenate(parts, axis=1)

        rim, far_rim = rims([widened_m(qm[h, f], h + 1, f) for f in range(fields)])
        return main, added(rim, 0), added(far_rim, 1)

    def tile_images(seen):
        high = seen.astype(bf16).astype(f32)
        both = jnp.where(pos_sub < CAP, high, seen - high)
        acc = None
        for t in range(tile_n):
            term = jnp.dot(spread(both, t), gram[t], preferred_element_type=f32)
            acc = term if acc is None else acc + term
        swapped = pltpu.roll(acc.reshape(lon_n, SLOT_ROWS, patch), CAP, 1)
        return acc + swapped.reshape(pos_n, patch)

    received(0)

    def power(it, carry, ratio=None):
        seen = seen_s[...] if ratio is None else ratio * seen_s[...]
        images = tile_images(seen)
        y_put(it + 1, images, ratio is None)
        y_start(it + 1, ratio is None)
        main, rim, far_rim = assembled(it)
        if ratio is not None:
            main, rim, far_rim = [ratio * v for v in main], ratio * rim, ratio * far_rim
        for f in range(fields):
            vecs[it, f] = main[f]
        vec_m[0], vec_m[1] = rim, far_rim
        main = [vecs[it, f] for f in range(fields)]
        rim, far_rim = vec_m[0], vec_m[1]
        first = first_pass(main, rim)
        u = [mixed(first, f)[:, center] for f in range(fields)]
        even = jnp.zeros((1, 128), f32)
        odd = lanes_of(jnp.where(pos_sub < CAP, seen * images, 0.0))
        for f in range(fields):
            here = main[f][:, center]
            even = even + lanes_of(here * here)
            odd = odd + lanes_of(u[f] * first[f][:, center])
        total_start(it, jnp.concatenate([even, odd], axis=1))
        second_pass(it + 1, first, rim_pass(main, rim, far_rim))
        if ratio is None:
            send_q(it + 1)
            received(it + 1)
        return carry

    lax.fori_loop(0, ITERS - 1, power, 0)
    m0, m1 = total(0)
    tau = m0 / m1
    power(ITERS - 1, 0, tau)
    wait_rows(y_rows, near_recv.at[ITERS])
    blocks = jnp.dot(
        own_oh[0:patch_n, :], yr[ITERS].reshape(own_k, patch), preferred_element_type=f32
    )

    m2, m3 = total(1)
    scale = 1.0 / m0
    g2, g3 = tau * tau * m2 * scale, tau * tau * tau * m3 * scale
    beta0 = g2 - 1.0
    c0 = 1.0 + beta0
    alpha1 = beta0 / (c0 * c0 - 2.0 * c0 * g2 + g3)
    a1, a2 = -1.0 - alpha1 * c0, alpha1
    m4, m5 = total(2)
    g4, g5 = tau * tau * m4 * scale, tau * tau * tau * m5 * scale
    gamma2 = 1.0 + 2.0 * a1 + (a1 * a1 + 2.0 * a2) * g2 + 2.0 * a1 * a2 * g3 + a2 * a2 * g4
    beta1 = gamma2 / beta0
    b0, b1, b2 = 1.0 + beta1 * c0, a1 - beta1, a2
    alpha2 = gamma2 / (
        b0 * b0
        + 2.0 * b0 * b1 * g2
        + (b1 * b1 + 2.0 * b0 * b2) * g3
        + 2.0 * b1 * b2 * g4
        + b2 * b2 * g5
    )
    x0, x1, x2 = (
        tau * (1.0 + alpha1 * c0 + alpha2 * b0),
        tau * tau * (alpha2 * b1 - alpha1),
        tau * tau * (alpha2 * b2),
    )
    r1, r2, r3 = tau * (a1 - alpha2 * b0), tau * (a2 - alpha2 * b1), -tau * tau * (alpha2 * b2)
    for f in range(fields):
        e0, e1, e2 = (vecs[it, f, :, center] for it in range(ITERS))
        sol_out[f] = x0 * e0 + x1 * e1 + x2 * e2
        res_out[f] = e0 + r1 * e1 + r2 * e2 + r3 * (qs[ITERS, f] + placed_field(blocks, f))

    @pl.when(inner)
    def _():
        wait_rows(sent_rows(sizes, bg.shape, patch), sent.at[0])

    @pl.when(jnp.logical_not(inner))
    def _():
        unsent = (ITERS + 1) * 4 + ((3 + ITERS) * band_rows + ITERS * msg_rows) // 2
        wait_rows(sent_rows(sizes, bg.shape, patch) - unsent, sent.at[0])


def sent_rows(sizes, shape, patch):
    lon_n, lat_n, fld_n = sizes
    fields, rows, cols = shape
    dev_n, pos_n = lon_n * lat_n * fld_n, lon_n * SLOT_ROWS
    halos = (ITERS + 1) * (2 * rows + 8) + (3 + ITERS) * 4 * fields * cols // 128
    asks = (lon_n - 1) * SLOT_ROWS + 3 * lon_n - 1
    inputs = ITERS * (lon_n - 1) * CAP * patch // 128
    images = (ITERS + 1) * (lon_n - 1) * pos_n * patch // 256
    rims = ITERS * 2 * lon_n * 2 * SLOT_ROWS * patch // 256
    return halos + asks + inputs + images + rims + ITERS * (dev_n - 1) * 2


def on_device(
    sizes,
    background,
    decay_sq,
    edge_weight,
    coupling,
    obs_tiles,
    obs_values,
    obs_weights,
    obs_counts,
    swath_ids,
    swath_scale,
    tile_owner,
    tile_slot,
):
    fields, rows, cols = background.shape
    tile_n, obs_len, patch = obs_tiles.shape
    lon_n, lat_n, fld_n = sizes
    dev_n = lon_n * lat_n * fld_n
    ext = cols + 2 * EDGE
    pos_n = lon_n * SLOT_ROWS
    patch_n = fields * rows * cols // patch
    side_n = 2 * fields * rows
    halos = ITERS + 1
    f32, bf16, i32 = jnp.float32, jnp.bfloat16, jnp.int32
    vmem = pl.BlockSpec(memory_space=pltpu.VMEM)
    dma = pltpu.SemaphoreType.DMA
    shape = pltpu.VMEM((fields, rows, cols), f32)
    block = pltpu.VMEM((fields, rows, ext), f32)
    return pl.pallas_call(
        functools.partial(kernel, sizes),
        out_shape=(shape, shape),
        in_specs=[pl.BlockSpec(memory_space=pltpu.HBM)] * 12,
        out_specs=(vmem, vmem),
        scratch_shapes=[
            pltpu.SMEM(tile_owner.shape, i32),
            pltpu.SMEM(tile_slot.shape, i32),
            pltpu.SMEM(obs_counts.shape, i32),
            pltpu.SMEM(swath_ids.shape, i32),
            pltpu.SMEM(swath_scale.shape, f32),
            pltpu.SMEM(coupling.shape, f32),
            pltpu.VMEM(background.shape, f32),
            pltpu.VMEM(decay_sq.shape, f32),
            pltpu.VMEM(edge_weight.shape, f32),
            pltpu.VMEM(obs_values.shape, f32),
            pltpu.VMEM(obs_weights.shape, f32),
            pltpu.VMEM((tile_n, obs_len, patch), bf16),
            pltpu.VMEM((tile_n, patch, patch), bf16),
            pltpu.VMEM((2 * tile_n, obs_len), bf16),
            pltpu.VMEM((tile_n, obs_len), f32),
            pltpu.VMEM((pos_n, patch), i32),
            pltpu.VMEM((8, rows, ext), f32),
            pltpu.VMEM((8, rows, ext), f32),
            block,
            pltpu.VMEM((rows, ext), f32),
            pltpu.VMEM((ITERS, fields, rows, ext), f32),
            pltpu.VMEM((2, rows, ext), f32),
            pltpu.VMEM((ITERS + 1, fields, rows, cols), f32),
            pltpu.VMEM((ITERS, fields, rows, cols), f32),
            pltpu.VMEM((3, fields, rows, cols), f32),
            pltpu.VMEM((halos, 2, rows, EDGE), f32),
            pltpu.VMEM((halos, 2, rows, EDGE), f32),
            pltpu.VMEM((halos, 2, rows, EDGE), f32),
            pltpu.VMEM((lon_n, SLOT_ROWS, 128), i32),
            pltpu.VMEM((lon_n, SLOT_ROWS, 128), i32),
            pltpu.VMEM((1, 128), i32),
            pltpu.VMEM((3 * lon_n, 1, 128), i32),
            pltpu.VMEM((pos_n, patch_n), bf16),
            pltpu.VMEM((patch_n + side_n + pos_n, lon_n * pos_n), bf16),
            pltpu.VMEM((2 * rows * (cols // patch) + 4 * rows, 4 * lon_n * SLOT_ROWS), bf16),
            pltpu.VMEM((ITERS, lon_n, SLOT_ROWS, patch), f32),
            pltpu.VMEM((ITERS, lon_n, SLOT_ROWS, patch), f32),
            pltpu.VMEM((ITERS + 1, pos_n, patch), bf16),
            pltpu.VMEM((ITERS + 1, lon_n, pos_n, patch), bf16),
            pltpu.VMEM((ITERS, lon_n, 2 * SLOT_ROWS, patch), bf16),
            pltpu.VMEM((ITERS, 2, lon_n, 2 * SLOT_ROWS, patch), bf16),
            pltpu.VMEM((ITERS, 1, 256), f32),
            pltpu.VMEM((ITERS, dev_n, 1, 256), f32),
            pltpu.VMEM((pos_n, patch), f32),
            pltpu.VMEM((patch_n + side_n + pos_n, patch), f32),
            pltpu.VMEM((sent_rows(sizes, background.shape, patch), 128), f32),
            dma((1,)),
            dma((1,)),
            dma((1,)),
            dma((ITERS + 1,)),
            dma((ITERS,)),
            dma((ITERS,)),
            dma((10,)),
        ],
        compiler_params=pltpu.CompilerParams(
            collective_id=0, has_side_effects=True, vmem_limit_bytes=67043328 - 3 * 2**20
        ),
    )(
        tile_owner,
        tile_slot,
        obs_counts,
        swath_ids,
        swath_scale,
        coupling,
        background,
        decay_sq,
        edge_weight,
        obs_tiles,
        obs_values,
        obs_weights,
    )


def solution(mesh):
    sizes = (mesh.shape["lon"], mesh.shape["lat"], mesh.shape["fld"])
    return jax.shard_map(
        functools.partial(on_device, sizes),
        mesh=mesh,
        in_specs=(
            P("group", ("lat", "fld"), "lon"),
            P(None, ("lat", "fld"), "lon"),
            P(None, ("lat", "fld"), "lon"),
            P(),
            P(("lon", "lat", "fld"), None, None),
            P(("group", "lon", "lat", "fld"), None),
            P(("lon", "lat", "fld"), None),
            P(("lon", "lat", "fld")),
            P(("lon", "lat", "fld")),
            P(),
            P(("lon", "lat", "fld")),
            P(("lon", "lat", "fld")),
        ),
        out_specs=(P("group", ("lat", "fld"), "lon"), P("group", ("lat", "fld"), "lon")),
        check_vma=False,
    )
```

```python
import functools

import jax
import jax.numpy as jnp
from jax import lax
from jax.experimental import pallas as pl
from jax.experimental.pallas import tpu as pltpu
from jax.sharding import PartitionSpec as P

CAP = 4
ITERS = 3
SLOT_ROWS = 8
EDGE = 128
GRAMS_AHEAD = 2
GRAMS_NEXT = 12
MESH = pl.DeviceIdType.MESH


def loop(low, high, body):
    if high - low <= 16:
        for k in range(low, high):
            body(k)
    else:
        lax.fori_loop(low, high, lambda k, c: (body(k), c)[1], 0)


def kernel(
    sizes,
    owner_hbm,
    slot_hbm,
    counts_hbm,
    swath_hbm,
    scale_hbm,
    coupling_hbm,
    bg_hbm,
    decay_hbm,
    edge_hbm,
    tiles_hbm,
    values_hbm,
    weights_hbm,
    sol_out,
    res_out,
    owner_s,
    slot_s,
    counts_s,
    swath_s,
    scale_s,
    coupling_s,
    bg,
    decay,
    edge,
    obs_values,
    obs_weights,
    tiles,
    gram,
    w_parts,
    q_rows,
    tile_of,
    coef,
    coef_m,
    diag,
    diag_m,
    vecs,
    vec_m,
    qs,
    qm,
    raw_m,
    pk_out,
    pk_in,
    pkm_in,
    ask,
    req,
    ask_row,
    req_row,
    gather_oh,
    own_oh,
    rim_oh,
    xs,
    xr,
    yv,
    yr,
    msg,
    msg_in,
    part,
    parts,
    seen_s,
    blocks_s,
    bytes_of,
    sent,
    halo_recv,
    ask_recv,
    near_recv,
    rim_recv,
    red_recv,
    load_sem,
):
    lon_n, lat_n, fld_n = sizes
    row_n = lat_n * fld_n
    dev_n = lon_n * row_n
    fields, rows, cols = bg.shape
    tile_n, obs_len, patch = tiles.shape
    ext = cols + 2 * EDGE
    per_row = cols // patch
    patch_n = fields * rows * per_row
    pos_n = lon_n * SLOT_ROWS
    bf16, f32, i32 = jnp.bfloat16, jnp.float32, jnp.int32

    my_lon = lax.axis_index("lon")
    my_row = lax.axis_index("lat") * fld_n + lax.axis_index("fld")
    me = my_lon * row_n + my_row

    def device(lon, row):
        return {"lon": lon, "lat": row // fld_n, "fld": row % fld_n}

    west, east = (my_lon + lon_n - 1) % lon_n, (my_lon + 1) % lon_n
    north, south = (my_row + row_n - 1) % row_n, (my_row + 1) % row_n
    has_north = my_row > 0
    has_south = my_row < row_n - 1
    inner = has_north & has_south

    loads = [
        pltpu.make_async_copy(src, dst, load_sem.at[k])
        for k, src, dst in (
            (0, owner_hbm, owner_s),
            (1, slot_hbm, slot_s),
            (2, counts_hbm, counts_s),
            (3, swath_hbm, swath_s),
            (4, scale_hbm, scale_s),
            (5, coupling_hbm, coupling_s),
            (6, values_hbm, obs_values),
            (7, weights_hbm, obs_weights),
            (8, tiles_hbm, tiles),
            (9, edge_hbm, edge),
            (9, bg_hbm, bg),
            (9, decay_hbm, decay),
        )
    ]
    for load in loads:
        load.start()

    barrier = pltpu.get_barrier_semaphore()

    def greet(k):
        other = (me + k) % dev_n
        pl.semaphore_signal(
            barrier, inc=1, device_id=device(other // row_n, other % row_n), device_id_type=MESH
        )

    for side, there in ((0, has_north), (1, has_south)):

        @pl.when(jnp.logical_not(there))
        def _():
            for i in range(ITERS):
                msg_in[i, side] = jnp.zeros(msg_in.shape[2:], bf16)

    loop(1, dev_n, greet)

    center = slice(EDGE, EDGE + cols)
    lane8 = lax.broadcasted_iota(i32, (rows, EDGE), 1)
    sub_e = lax.broadcasted_iota(i32, (rows, ext), 0)
    top, bottom = sub_e == 0, sub_e == rows - 1
    low_half = sub_e < fields
    rim_mask = (low_half & has_north) | ((sub_e >= fields) & has_south)
    edge_mask = ((sub_e < 2) & has_south) | ((sub_e >= rows - 2) & has_north)

    toward = jnp.where(my_lon < lon_n // 2, lon_n - 1, 1)

    def remote_start(src, dst, recv_sem, lon, row):
        pltpu.make_async_remote_copy(
            src_ref=src,
            dst_ref=dst,
            send_sem=sent.at[0],
            recv_sem=recv_sem,
            device_id=device(lon, row),
            device_id_type=MESH,
        ).start()

    def wait_rows(count, sem):
        some = bytes_of.at[pl.ds(0, count)]
        pltpu.make_async_copy(some, some, sem).wait()

    band_rows = 2 * fields * 2 * cols // 128
    pack_rows = 2 * rows + 4 * 2
    x_rows = (lon_n - 1) * CAP * patch // 128
    y_rows = (lon_n - 1) * pos_n * patch // 256
    msg_rows = 2 * lon_n * 2 * SLOT_ROWS * patch // 256
    ask_rows = (lon_n - 1) * SLOT_ROWS + 3 * lon_n - 1
    sum_rows = (dev_n - 1) * 2

    def turn(value, by):
        return pltpu.roll(value, by % EDGE, 1) if by % EDGE else value

    first_two, last_two = pl.ds(0, 2), pl.ds(rows - 2, 2)

    def halo_start(h):
        pairs = [
            (pk_out.at[h, 0], pk_in.at[h, 1], west, my_row),
            (pk_out.at[h, 1], pk_in.at[h, 0], east, my_row),
            (pk_out.at[h, 0, first_two], pkm_in.at[h, 1, first_two], west, north),
            (pk_out.at[h, 1, first_two], pkm_in.at[h, 0, first_two], east, north),
            (pk_out.at[h, 0, last_two], pkm_in.at[h, 1, last_two], west, south),
            (pk_out.at[h, 1, last_two], pkm_in.at[h, 0, last_two], east, south),
        ]
        if isinstance(h, int) and h == 0:
            bands = [(bg, raw_m.at[0]), (edge, raw_m.at[1]), (decay, raw_m.at[2])]
        else:
            bands = [(qs.at[h - 1], qm.at[h - 1])]
        for src, dst in bands:
            near_count = 1 if src is decay else 2
            low_rows, high_rows = pl.ds(0, near_count), pl.ds(rows - near_count, near_count)
            for f in range(fields):
                pairs.append((src.at[f, low_rows], dst.at[f, low_rows], my_lon, north))
                pairs.append((src.at[f, high_rows], dst.at[f, high_rows], my_lon, south))
        sem = halo_recv.at[0] if isinstance(h, int) and h == 0 else rim_recv.at[h - 1]
        for src, dst, lon, row in pairs[:2]:
            remote_start(src, dst, sem, lon, row)

        @pl.when(has_north)
        def _():
            for src, dst, lon, row in pairs[2:]:
                if row is north:
                    remote_start(src, dst, sem, lon, row)

        @pl.when(has_south)
        def _():
            for src, dst, lon, row in pairs[2:]:
                if row is south:
                    remote_start(src, dst, sem, lon, row)

    def pack(h, values):
        to_west = jnp.zeros((rows, EDGE), f32)
        to_east = to_west
        for g, value in enumerate(values):
            here = lane8 // 2 == g
            to_west = jnp.where(here, turn(value[:, 0:EDGE], 2 * g), to_west)
            to_east = jnp.where(here, turn(value[:, cols - EDGE : cols], 2 * g + 2), to_east)
        pk_out[h, 0] = to_west
        pk_out[h, 1] = to_east

    def west_part(buffer, h, g):
        return turn(buffer[h, 0], EDGE - 2 - 2 * g)

    def east_part(buffer, h, g):
        return turn(buffer[h, 1], EDGE - 2 * g)

    def widened(value, h, g):
        return jnp.concatenate([west_part(pk_in, h, g), value, east_part(pk_in, h, g)], axis=1)

    def widened_m(value, h, g):
        return jnp.concatenate([west_part(pkm_in, h, g), value, east_part(pkm_in, h, g)], axis=1)

    def packed(values, north_row, south_row):
        out = pltpu.roll(values[0], -north_row % rows, 0)
        for f in range(1, fields):
            out = jnp.where(sub_e == f, pltpu.roll(values[f], (f - north_row) % rows, 0), out)
        for f in range(fields):
            moved = pltpu.roll(values[f], (fields + f - south_row) % rows, 0)
            out = jnp.where(sub_e == fields + f, moved, out)
        return out

    def rims(values):
        near_rim = packed(values, rows - 1, 0)
        far_rim = packed(values, rows - 2, 1)
        return jnp.where(rim_mask, near_rim, 0.0), jnp.where(rim_mask, far_rim, 0.0)

    def y_put(i, value, with_rim=True):
        pos_half = lax.broadcasted_iota(i32, (pos_n, patch), 0) % SLOT_ROWS < CAP
        high = value.astype(bf16).astype(f32)
        both = jnp.where(pos_half, high, value - high)
        full = both.astype(bf16)
        yv[i] = full
        yr[i, my_lon] = full
        if with_rim:
            blocks = [both[l * SLOT_ROWS : (l + 1) * SLOT_ROWS] for l in range(lon_n)]
            for l in range(lon_n):
                rim = jnp.concatenate(
                    [blocks[l - 1][:, patch - EDGE :], blocks[(l + 1) % lon_n][:, :EDGE]], axis=1
                )
                msg[i, l] = jnp.concatenate([blocks[l], rim], axis=0).astype(bf16)

    def y_start(i, with_rim=True):
        def send(k):
            remote_start(
                yv.at[i], yr.at[i, my_lon], near_recv.at[i], (my_lon + k * toward) % lon_n, my_row
            )

        loop(1, lon_n, send)
        if with_rim:

            def send_rim(k):
                to = (my_lon + k * toward) % lon_n

                @pl.when(has_north)
                def _():
                    remote_start(msg.at[i, to], msg_in.at[i, 1, my_lon], rim_recv.at[i], to, north)

                @pl.when(has_south)
                def _():
                    remote_start(msg.at[i, to], msg_in.at[i, 0, my_lon], rim_recv.at[i], to, south)

            loop(0, lon_n, send_rim)

    def x_start(i):
        def send(k):
            to = (my_lon + k * toward) % lon_n
            remote_start(
                xs.at[i, to, pl.ds(0, CAP)],
                xr.at[i, my_lon, pl.ds(0, CAP)],
                near_recv.at[i],
                to,
                my_row,
            )

        loop(1, lon_n, send)

    def total_start(k, value):
        part[k] = value
        parts[k, me] = value

        def send(j):
            lon = (my_lon + (j // row_n + 1) * toward) % lon_n
            row = (my_row + j % row_n + row_n // 2) % row_n
            remote_start(part.at[k], parts.at[k, me], red_recv.at[k], lon, row)

        def send_along(j):
            row = (my_row + j) % row_n
            remote_start(part.at[k], parts.at[k, me], red_recv.at[k], my_lon, row)

        loop(0, (lon_n - 1) * row_n, send)
        loop(1, row_n, send_along)

    def total(k):
        wait_rows(sum_rows, red_recv.at[k])
        sums = jnp.sum(parts[k], axis=0)
        return (
            jnp.sum(sums[:, 0:128], axis=1, keepdims=True),
            jnp.sum(sums[:, 128:256], axis=1, keepdims=True),
        )

    def lanes_of(value):
        lane_sum = value[:, 0:128]
        for k in range(1, value.shape[1] // 128):
            lane_sum = lane_sum + value[:, k * 128 : (k + 1) * 128]
        return jnp.sum(lane_sum, axis=0, keepdims=True)

    def mixed(values, f):
        acc = coupling_s[f, 0] * values[0]
        for g in range(1, fields):
            acc = acc + coupling_s[f, g] * values[g]
        return acc

    for load in loads[:8]:
        load.wait()

    pos_row = lax.broadcasted_iota(i32, (pos_n, 128), 0)
    row_lane = lax.broadcasted_iota(i32, (8, 128), 1)
    tile_row = lax.broadcasted_iota(i32, (tile_n, obs_len), 0)
    obs_lane = lax.broadcasted_iota(i32, (tile_n, obs_len), 1)
    holds = jnp.full((pos_n, 128), -1, i32)
    asked = jnp.full((pos_n, 128), -2, i32)
    asked_row = jnp.full((8, 128), -1, i32)
    scale_of = jnp.zeros((tile_n, obs_len), f32)
    count_of = jnp.zeros((tile_n, obs_len), i32)
    for t in range(tile_n):
        rank = jnp.int32(0)
        for other in range(t):
            rank = rank + (owner_s[other] == owner_s[t]).astype(i32)
        number = slot_s[t]
        column, rest = number % per_row, number // per_row
        moved = (column * fields + rest // rows) * rows + rest % rows
        place = owner_s[t] * SLOT_ROWS + rank
        here = (pos_row == place) | (pos_row == place + CAP)
        here_row = (row_lane == place) | (row_lane == place + CAP)
        holds = jnp.where(here, t, holds)
        asked = jnp.where(here, moved, asked)
        asked_row = jnp.where(here_row, moved, asked_row)
        scale_of = jnp.where(tile_row == t, scale_s[swath_s[t]], scale_of)
        count_of = jnp.where(tile_row == t, counts_s[t], count_of)
    tile_of[...] = jnp.concatenate([holds] * (patch // 128), axis=1)
    ask[...] = asked.reshape(lon_n, SLOT_ROWS, 128)
    req[my_lon] = ask[my_lon]
    ask_row[...] = asked_row[0:1]
    req_row[lon_n + my_lon] = asked_row[0:1]
    weight = jnp.where(obs_lane < count_of, obs_weights[...] * scale_of, 0.0)
    weight_high = weight.astype(bf16).astype(f32)
    w_parts[...] = jnp.concatenate([weight_high, weight - weight_high], axis=0).astype(bf16)
    q_rows[...] = (weight * obs_values[...]).astype(bf16).astype(f32)

    def spread(value, t):
        return jnp.where(tile_of[...] == t, value, 0.0).astype(bf16)

    loads[8].wait()
    acc = None
    for t in range(tile_n):
        term = jnp.dot(
            spread(q_rows[t : t + 1, :], t), tiles[t], preferred_element_type=f32
        )
        acc = term if acc is None else acc + term
    y_put(0, acc)

    pick_row = lax.broadcasted_iota(i32, (2 * tile_n, 128), 0) % tile_n

    def gram_of(t, carry):
        chosen = jnp.where(pick_row == t, 1.0, 0.0).astype(bf16)
        column = lax.dot_general(
            w_parts[...], chosen, (((0,), (0,)), ((), ())), preferred_element_type=f32
        )
        tile = tiles[t]
        scaled = (tile.astype(f32) * jnp.concatenate([column] * (patch // 128), axis=1)).astype(bf16)
        gram[t] = lax.dot_general(
            tile, scaled, (((0,), (0,)), ((), ())), preferred_element_type=f32
        ).astype(bf16)
        return carry

    lax.fori_loop(0, GRAMS_AHEAD, gram_of, 0)

    pltpu.make_async_copy(raw_m, raw_m, load_sem.at[9]).wait()
    pack(0, [bg[f] for f in range(fields)] + [edge[e] for e in range(4)] + [decay[f] for f in range(fields)])

    pl.semaphore_wait(barrier, dev_n - 1)
    halo_start(0)

    def send_ask(k):
        to = (my_lon + k * toward) % lon_n
        remote_start(ask.at[to], req.at[my_lon], ask_recv.at[0], to, my_row)
        remote_start(ask_row, req_row.at[lon_n + my_lon], ask_recv.at[0], to, my_row)

    def send_ask_rim(k):
        to = (my_lon + k * toward) % lon_n
        remote_start(ask_row, req_row.at[2 * lon_n + my_lon], ask_recv.at[0], to, north)
        remote_start(ask_row, req_row.at[my_lon], ask_recv.at[0], to, south)

    loop(1, lon_n, send_ask)
    loop(0, lon_n, send_ask_rim)

    y_start(0)
    lax.fori_loop(GRAMS_AHEAD, GRAMS_NEXT, gram_of, 0)


    @pl.when(inner)
    def _():
        wait_rows(pack_rows + 5 * band_rows // 2, halo_recv.at[0])

    @pl.when(jnp.logical_not(inner))
    def _():
        wait_rows(pack_rows - 4 + 5 * band_rows // 4, halo_recv.at[0])

    w = [widened(edge[e], 0, 4 + e) for e in range(4)]
    wm = [jnp.where(edge_mask, widened_m(raw_m[1, e], 0, 4 + e), 0.0) for e in range(4)]

    def around(main, rim):
        m1, r1 = pltpu.roll(main, 1, 0), pltpu.roll(rim, 1, 0)
        m7, r7 = pltpu.roll(main, rows - 1, 0), pltpu.roll(rim, rows - 1, 0)
        return (
            jnp.where(top, r1, m1),
            jnp.where(bottom, r7, m7),
            jnp.where(top, m1, r1),
            jnp.where(bottom, m7, r7),
        )

    near = [around(w[e], wm[e]) for e in range(4)]

    def coefficients(here, up, down):
        w_west = {e: pltpu.roll(here[e], 1, 1) for e in (0, 2, 3)}
        w_east = {e: pltpu.roll(here[e], ext - 1, 1) for e in (0, 2, 3)}
        e0, e1, e2 = (
            0.5 * (w_west[0] + here[0]),
            0.5 * (w_west[3] + up[3]),
            0.5 * (w_west[2] + down[2]),
        )
        v0, v1, v2 = (
            0.5 * (w_east[0] + here[0]),
            0.5 * (w_east[2] + up[2]),
            0.5 * (w_east[3] + down[3]),
        )
        n0, n1 = 0.5 * (here[1] + up[1]), 0.5 * (here[1] + down[1])
        degree = (
            n0 + n1 + pltpu.roll(e0 + e1 + e2, ext - 1, 1) + pltpu.roll(v0 + v1 + v2, 1, 1)
        )
        return (e0, e1, e2, v0, v1, v2, n0, n1), degree

    values, degree = coefficients(
        w, [near[e][0] for e in range(4)], [near[e][1] for e in range(4)]
    )
    for k, value in enumerate(values):
        coef[k] = value
    for f in range(fields):
        diag[f] = widened(decay[f], 0, 8 + f) + degree
    values, degree = coefficients(
        wm, [near[e][2] for e in range(4)], [near[e][3] for e in range(4)]
    )
    for k, value in enumerate(values):
        coef_m[k] = jnp.where(low_half, value[rows - 1 : rows], value[0:1])
    diag_m[...] = packed(
        [widened_m(raw_m[2, f], 0, 8 + f) + degree for f in range(fields)], rows - 1, 0
    )

    def apply_l(c, d, value, up, down):
        toward_east = c[0] * value + c[1] * up + c[2] * down
        toward_west = c[3] * value + c[4] * up + c[5] * down
        result = d * value - c[6] * up - c[7] * down
        return result - pltpu.roll(toward_east, ext - 1, 1) - pltpu.roll(toward_west, 1, 1)

    lane_row = lax.broadcasted_iota(i32, (rows, 128), 0)
    blends = []
    for d in range(fields):
        blend = jnp.zeros((rows, 128), f32)
        for k in range(rows):
            blend = jnp.where(lane_row == k, coupling_s[k % fields, (k + d) % fields], blend)
        blends.append(jnp.concatenate([blend] * (ext // 128), axis=1))

    def mixed_rim(value):
        acc = blends[0] * value
        for d in range(1, fields):
            ahead = pltpu.roll(value, rows - d, 0)
            behind = pltpu.roll(value, fields - d, 0)
            acc = acc + blends[d] * jnp.where(sub_e % fields < fields - d, ahead, behind)
        return acc

    def beside(value, rim, f):
        up = jnp.where(top, pltpu.roll(rim, -f % rows, 0), pltpu.roll(value, 1, 0))
        down = jnp.where(
            bottom, pltpu.roll(rim, (fields - 1 - f) % rows, 0), pltpu.roll(value, rows - 1, 0)
        )
        return up, down

    def first_pass(main, rim):
        return [
            apply_l(coef, diag[f], main[f], *beside(main[f], rim, f)) for f in range(fields)
        ]

    def rim_pass(main, rim, far_rim):
        inside = packed(main, 0, rows - 1)
        up = jnp.where(low_half, far_rim, inside)
        down = jnp.where(low_half, inside, far_rim)
        return apply_l(coef_m, diag_m[...], rim, up, down)

    def second_pass(h, first, first_rim):
        u = [mixed(first, f) for f in range(fields)]
        u_rim = jnp.where(rim_mask, mixed_rim(first_rim), 0.0)
        for f in range(fields):
            qs[h, f] = apply_l(coef, diag[f], u[f], *beside(u[f], u_rim, f))[:, center]

    def send_q(h):
        pack(h + 1, [qs[h, f] for f in range(fields)])
        stacked = jnp.concatenate(
            [
                qs[h, f, :, c * patch : (c + 1) * patch]
                for c in range(per_row)
                for f in range(fields)
            ],
            axis=0,
        )
        high = stacked.astype(bf16)
        low = (stacked - high.astype(f32)).astype(bf16)
        chosen = gather_oh[...]
        patches = jnp.dot(chosen, low, preferred_element_type=f32) + jnp.dot(
            chosen, high, preferred_element_type=f32
        )
        xs[h] = patches.reshape(lon_n, SLOT_ROWS, patch)
        x_start(h)
        halo_start(h + 1)
        xr[h, my_lon] = xs[h, my_lon]

    main = [widened(bg[f], 0, f) for f in range(fields)]
    rim, far_rim = rims([widened_m(raw_m[0, f], 0, f) for f in range(fields)])
    second_pass(0, first_pass(main, rim), rim_pass(main, rim, far_rim))

    wait_rows(ask_rows, ask_recv.at[0])
    wanted = req[...].reshape(pos_n, 128)
    wanted = jnp.concatenate([wanted] * (patch_n // 128), axis=1)
    picked = wanted == lax.broadcasted_iota(i32, (pos_n, patch_n), 1)
    gather_oh[...] = jnp.where(picked, 1.0, 0.0).astype(bf16)
    send_q(0)

    lane1 = lax.broadcasted_iota(i32, (1, 128), 1)
    own_k, rim_k = lon_n * pos_n, 2 * lon_n * 2 * SLOT_ROWS

    def iota(n, axis):
        return lax.broadcasted_iota(i32, (n, 128), axis)

    own_rows = iota(patch_n, 0)
    side_rows = iota(fields * rows, 0)
    for group in range(own_k // 128):
        slots = jnp.full((1, 128), -1, i32)
        for h in range(lon_n):
            if h * pos_n // 128 == group:
                offset = h * pos_n % 128
                moved = turn(req_row[lon_n + h], offset)
                slots = jnp.where((lane1 >= offset) & (lane1 < offset + pos_n), moved, slots)
        lanes = slice(group * 128, (group + 1) * 128)
        at = lane1 % pos_n // SLOT_ROWS

        def match(rows_of, owner):
            wanted = jnp.where(at == owner, slots, -1)
            return jnp.where(rows_of == wanted, 1.0, 0.0).astype(bf16)

        own_oh[0:patch_n, lanes] = match(own_rows, my_lon)
        first_side, last_side = patch_n, patch_n + fields * rows
        own_oh[first_side:last_side, lanes] = match(
            (per_row - 1) * fields * rows + side_rows, west
        )
        own_oh[last_side : last_side + fields * rows, lanes] = match(side_rows, east)
        tile_rows = last_side + fields * rows
        mine = (iota(pos_n, 0) // SLOT_ROWS == at) & (ask[...].reshape(pos_n, 128) == slots)
        own_oh[tile_rows : tile_rows + pos_n, lanes] = jnp.where(mine, 1.0, 0.0).astype(bf16)

    for group in range(rim_k // 128):
        ours = jnp.full((1, 128), -1, i32)
        from_west, from_east = ours, ours
        side = group * 128 // (rim_k // 2)
        for index in range(2 * lon_n):
            if index * 2 * SLOT_ROWS // 128 != group:
                continue
            offset = index * 2 * SLOT_ROWS % 128
            table = jnp.broadcast_to(
                req_row[(index // lon_n) * 2 * lon_n + index % lon_n], (8, 128)
            )
            low = (lane1 >= offset) & (lane1 < offset + SLOT_ROWS)
            high = (lane1 >= offset + SLOT_ROWS) & (lane1 < offset + 2 * SLOT_ROWS)

            def brought(owner, to):
                by = (to - owner * SLOT_ROWS + 2 * 128) % 128
                return pltpu.roll(table, by, 1)[0:1]

            ours = jnp.where(low, brought(my_lon, offset), ours)
            from_west = jnp.where(high, brought(west, offset + SLOT_ROWS), from_west)
            from_east = jnp.where(high, brought(east, offset + SLOT_ROWS), from_east)
        lanes = slice(group * 128, (group + 1) * 128)
        is_north = (group * 128 + lane1) < rim_k // 2

        def match_rim(count, column, far, wanted):
            row = iota(count, 0)
            is_south = row % rows // fields
            line = jnp.where(is_south == 1, far, rows - 1 - far)
            number = ((row // rows + column) * fields + row % fields) * rows + line
            keep = (is_north & has_north & (is_south == 0)) | (
                (~is_north) & has_south & (is_south == 1)
            )
            return jnp.where(keep & (number == wanted), 1.0, 0.0)

        span = per_row * rows
        rim_oh[0:span, lanes] = match_rim(span, 0, 0, ours).astype(bf16)
        rim_oh[span : 2 * span, lanes] = match_rim(span, 0, 1, ours).astype(bf16)
        corners = [
            match_rim(rows, per_row - 1, 0, from_west),
            match_rim(rows, per_row - 1, 1, from_west),
            match_rim(rows, 0, 0, from_east),
            match_rim(rows, 0, 1, from_east),
        ]
        rim_oh[2 * span :, lanes] = jnp.concatenate(corners, axis=0).astype(bf16)

    lax.fori_loop(GRAMS_NEXT, tile_n, gram_of, 0)

    pos_sub = lax.broadcasted_iota(i32, (pos_n, patch), 0) % SLOT_ROWS

    def placed_field(blocks, f):
        return jnp.concatenate(
            [
                blocks[(c * fields + f) * rows : (c * fields + f + 1) * rows]
                for c in range(per_row)
            ],
            axis=1,
        )

    def received(h):
        wait_rows(x_rows + y_rows, near_recv.at[h])
        blocks = jnp.dot(
            own_oh[...], yr[h].reshape(own_k, patch), preferred_element_type=f32
        )
        came = xr[h].reshape(pos_n, patch)
        came = jnp.where(pos_sub < CAP, came, pltpu.roll(came, CAP, 0))
        seen = came + blocks[patch_n + 2 * fields * rows :]
        seen_s[...] = seen
        blocks_s[...] = blocks

    def assembled(h):
        blocks = blocks_s[...]

        @pl.when(inner)
        def _():
            wait_rows(pack_rows + band_rows + msg_rows, rim_recv.at[h])

        @pl.when(jnp.logical_not(inner))
        def _():
            wait_rows(pack_rows - 4 + (band_rows + msg_rows) // 2, rim_recv.at[h])

        rim_blocks = jnp.dot(
            rim_oh[...], msg_in[h].reshape(rim_k, patch), preferred_element_type=f32
        )
        main = []
        for f in range(fields):
            west_rows = slice(patch_n + f * rows, patch_n + (f + 1) * rows)
            east_rows = slice(patch_n + (fields + f) * rows, patch_n + (fields + f + 1) * rows)
            main.append(
                jnp.concatenate(
                    [
                        west_part(pk_in, h + 1, f) + blocks[west_rows, patch - EDGE :],
                        qs[h, f] + placed_field(blocks, f),
                        east_part(pk_in, h + 1, f) + blocks[east_rows, :EDGE],
                    ],
                    axis=1,
                )
            )
        corner = 2 * per_row * rows

        def added(value, far):
            parts = [rim_blocks[corner + far * rows : corner + (far + 1) * rows, :EDGE]]
            for c in range(per_row):
                start = (far * per_row + c) * rows
                parts.append(rim_blocks[start : start + rows])
            start = corner + (2 + far) * rows
            parts.append(rim_blocks[start : start + rows, patch - EDGE :])
            return value + jnp.concatenate(parts, axis=1)

        rim, far_rim = rims([widened_m(qm[h, f], h + 1, f) for f in range(fields)])
        return main, added(rim, 0), added(far_rim, 1)

    def tile_images(seen):
        high = seen.astype(bf16).astype(f32)
        both = jnp.where(pos_sub < CAP, high, seen - high)
        acc = None
        for t in range(tile_n):
            term = jnp.dot(spread(both, t), gram[t], preferred_element_type=f32)
            acc = term if acc is None else acc + term
        swapped = pltpu.roll(acc.reshape(lon_n, SLOT_ROWS, patch), CAP, 1)
        return acc + swapped.reshape(pos_n, patch)

    received(0)

    def power(it, carry, ratio=None):
        seen = seen_s[...] if ratio is None else ratio * seen_s[...]
        images = tile_images(seen)
        y_put(it + 1, images, ratio is None)
        y_start(it + 1, ratio is None)
        main, rim, far_rim = assembled(it)
        if ratio is not None:
            main, rim, far_rim = [ratio * v for v in main], ratio * rim, ratio * far_rim
        for f in range(fields):
            vecs[it, f] = main[f]
        vec_m[0], vec_m[1] = rim, far_rim
        main = [vecs[it, f] for f in range(fields)]
        rim, far_rim = vec_m[0], vec_m[1]
        first = first_pass(main, rim)
        u = [mixed(first, f)[:, center] for f in range(fields)]
        even = jnp.zeros((1, 128), f32)
        odd = lanes_of(jnp.where(pos_sub < CAP, seen * images, 0.0))
        for f in range(fields):
            here = main[f][:, center]
            even = even + lanes_of(here * here)
            odd = odd + lanes_of(u[f] * first[f][:, center])
        sums = jnp.concatenate([even, odd], axis=1)
        if ratio is not None:
            total_start(it, sums)
        second_pass(it + 1, first, rim_pass(main, rim, far_rim))
        if ratio is None:
            send_q(it + 1)
            total_start(it, sums)
            received(it + 1)
        return carry

    lax.fori_loop(0, ITERS - 1, power, 0)
    m0, m1 = total(0)
    tau = m0 / m1
    power(ITERS - 1, 0, tau)
    wait_rows(y_rows, near_recv.at[ITERS])
    blocks = jnp.dot(
        own_oh[0:patch_n, :], yr[ITERS].reshape(own_k, patch), preferred_element_type=f32
    )

    m2, m3 = total(1)
    scale = 1.0 / m0
    g2, g3 = tau * tau * m2 * scale, tau * tau * tau * m3 * scale
    beta0 = g2 - 1.0
    c0 = 1.0 + beta0
    alpha1 = beta0 / (c0 * c0 - 2.0 * c0 * g2 + g3)
    a1, a2 = -1.0 - alpha1 * c0, alpha1
    m4, m5 = total(2)
    g4, g5 = tau * tau * m4 * scale, tau * tau * tau * m5 * scale
    gamma2 = 1.0 + 2.0 * a1 + (a1 * a1 + 2.0 * a2) * g2 + 2.0 * a1 * a2 * g3 + a2 * a2 * g4
    beta1 = gamma2 / beta0
    b0, b1, b2 = 1.0 + beta1 * c0, a1 - beta1, a2
    alpha2 = gamma2 / (
        b0 * b0
        + 2.0 * b0 * b1 * g2
        + (b1 * b1 + 2.0 * b0 * b2) * g3
        + 2.0 * b1 * b2 * g4
        + b2 * b2 * g5
    )
    x0, x1, x2 = (
        tau * (1.0 + alpha1 * c0 + alpha2 * b0),
        tau * tau * (alpha2 * b1 - alpha1),
        tau * tau * (alpha2 * b2),
    )
    r1, r2, r3 = tau * (a1 - alpha2 * b0), tau * (a2 - alpha2 * b1), -tau * tau * (alpha2 * b2)
    for f in range(fields):
        e0, e1, e2 = (vecs[it, f, :, center] for it in range(ITERS))
        sol_out[f] = x0 * e0 + x1 * e1 + x2 * e2
        res_out[f] = e0 + r1 * e1 + r2 * e2 + r3 * (qs[ITERS, f] + placed_field(blocks, f))

    @pl.when(inner)
    def _():
        wait_rows(sent_rows(sizes, bg.shape, patch), sent.at[0])

    @pl.when(jnp.logical_not(inner))
    def _():
        unsent = (ITERS + 1) * 4 + ((5 + 2 * ITERS) * band_rows // 2 + ITERS * msg_rows) // 2
        wait_rows(sent_rows(sizes, bg.shape, patch) - unsent, sent.at[0])


def sent_rows(sizes, shape, patch):
    lon_n, lat_n, fld_n = sizes
    fields, rows, cols = shape
    dev_n, pos_n = lon_n * lat_n * fld_n, lon_n * SLOT_ROWS
    halos = (ITERS + 1) * (2 * rows + 8) + (5 + 2 * ITERS) * 2 * fields * cols // 128
    asks = (lon_n - 1) * SLOT_ROWS + 3 * lon_n - 1
    inputs = ITERS * (lon_n - 1) * CAP * patch // 128
    images = (ITERS + 1) * (lon_n - 1) * pos_n * patch // 256
    rims = ITERS * 2 * lon_n * 2 * SLOT_ROWS * patch // 256
    return halos + asks + inputs + images + rims + ITERS * (dev_n - 1) * 2


def on_device(
    sizes,
    background,
    decay_sq,
    edge_weight,
    coupling,
    obs_tiles,
    obs_values,
    obs_weights,
    obs_counts,
    swath_ids,
    swath_scale,
    tile_owner,
    tile_slot,
):
    fields, rows, cols = background.shape
    tile_n, obs_len, patch = obs_tiles.shape
    lon_n, lat_n, fld_n = sizes
    dev_n = lon_n * lat_n * fld_n
    ext = cols + 2 * EDGE
    pos_n = lon_n * SLOT_ROWS
    patch_n = fields * rows * cols // patch
    side_n = 2 * fields * rows
    halos = ITERS + 1
    f32, bf16, i32 = jnp.float32, jnp.bfloat16, jnp.int32
    vmem = pl.BlockSpec(memory_space=pltpu.VMEM)
    dma = pltpu.SemaphoreType.DMA
    shape = pltpu.VMEM((fields, rows, cols), f32)
    block = pltpu.VMEM((fields, rows, ext), f32)
    return pl.pallas_call(
        functools.partial(kernel, sizes),
        out_shape=(shape, shape),
        in_specs=[pl.BlockSpec(memory_space=pltpu.HBM)] * 12,
        out_specs=(vmem, vmem),
        scratch_shapes=[
            pltpu.SMEM(tile_owner.shape, i32),
            pltpu.SMEM(tile_slot.shape, i32),
            pltpu.SMEM(obs_counts.shape, i32),
            pltpu.SMEM(swath_ids.shape, i32),
            pltpu.SMEM(swath_scale.shape, f32),
            pltpu.SMEM(coupling.shape, f32),
            pltpu.VMEM(background.shape, f32),
            pltpu.VMEM(decay_sq.shape, f32),
            pltpu.VMEM(edge_weight.shape, f32),
            pltpu.VMEM(obs_values.shape, f32),
            pltpu.VMEM(obs_weights.shape, f32),
            pltpu.VMEM((tile_n, obs_len, patch), bf16),
            pltpu.VMEM((tile_n, patch, patch), bf16),
            pltpu.VMEM((2 * tile_n, obs_len), bf16),
            pltpu.VMEM((tile_n, obs_len), f32),
            pltpu.VMEM((pos_n, patch), i32),
            pltpu.VMEM((8, rows, ext), f32),
            pltpu.VMEM((8, rows, ext), f32),
            block,
            pltpu.VMEM((rows, ext), f32),
            pltpu.VMEM((ITERS, fields, rows, ext), f32),
            pltpu.VMEM((2, rows, ext), f32),
            pltpu.VMEM((ITERS + 1, fields, rows, cols), f32),
            pltpu.VMEM((ITERS, fields, rows, cols), f32),
            pltpu.VMEM((3, fields, rows, cols), f32),
            pltpu.VMEM((halos, 2, rows, EDGE), f32),
            pltpu.VMEM((halos, 2, rows, EDGE), f32),
            pltpu.VMEM((halos, 2, rows, EDGE), f32),
            pltpu.VMEM((lon_n, SLOT_ROWS, 128), i32),
            pltpu.VMEM((lon_n, SLOT_ROWS, 128), i32),
            pltpu.VMEM((1, 128), i32),
            pltpu.VMEM((3 * lon_n, 1, 128), i32),
            pltpu.VMEM((pos_n, patch_n), bf16),
            pltpu.VMEM((patch_n + side_n + pos_n, lon_n * pos_n), bf16),
            pltpu.VMEM((2 * rows * (cols // patch) + 4 * rows, 4 * lon_n * SLOT_ROWS), bf16),
            pltpu.VMEM((ITERS, lon_n, SLOT_ROWS, patch), f32),
            pltpu.VMEM((ITERS, lon_n, SLOT_ROWS, patch), f32),
            pltpu.VMEM((ITERS + 1, pos_n, patch), bf16),
            pltpu.VMEM((ITERS + 1, lon_n, pos_n, patch), bf16),
            pltpu.VMEM((ITERS, lon_n, 2 * SLOT_ROWS, patch), bf16),
            pltpu.VMEM((ITERS, 2, lon_n, 2 * SLOT_ROWS, patch), bf16),
            pltpu.VMEM((ITERS, 1, 256), f32),
            pltpu.VMEM((ITERS, dev_n, 1, 256), f32),
            pltpu.VMEM((pos_n, patch), f32),
            pltpu.VMEM((patch_n + side_n + pos_n, patch), f32),
            pltpu.VMEM((sent_rows(sizes, background.shape, patch), 128), f32),
            dma((1,)),
            dma((1,)),
            dma((1,)),
            dma((ITERS + 1,)),
            dma((ITERS,)),
            dma((ITERS,)),
            dma((10,)),
        ],
        compiler_params=pltpu.CompilerParams(
            collective_id=0, has_side_effects=True, vmem_limit_bytes=67043328 - 3 * 2**20
        ),
    )(
        tile_owner,
        tile_slot,
        obs_counts,
        swath_ids,
        swath_scale,
        coupling,
        background,
        decay_sq,
        edge_weight,
        obs_tiles,
        obs_values,
        obs_weights,
    )


def solution(mesh):
    sizes = (mesh.shape["lon"], mesh.shape["lat"], mesh.shape["fld"])
    return jax.shard_map(
        functools.partial(on_device, sizes),
        mesh=mesh,
        in_specs=(
            P("group", ("lat", "fld"), "lon"),
            P(None, ("lat", "fld"), "lon"),
            P(None, ("lat", "fld"), "lon"),
            P(),
            P(("lon", "lat", "fld"), None, None),
            P(("group", "lon", "lat", "fld"), None),
            P(("lon", "lat", "fld"), None),
            P(("lon", "lat", "fld")),
            P(("lon", "lat", "fld")),
            P(),
            P(("lon", "lat", "fld")),
            P(("lon", "lat", "fld")),
        ),
        out_specs=(P("group", ("lat", "fld"), "lon"), P("group", ("lat", "fld"), "lon")),
        check_vma=False,
    )
```
